256 devices in a mesh: row: 16 (over y_lo, z), col: 16 (over y_hi, x, core).
Axes of the slice: x: 4, y: 4 (y_hi: 2, y_lo: 2; y = y_hi * 2 + y_lo), z: 8, core: 2. Of those that a mesh axis runs over, the one named last changes fastest.
Arguments:
- hidden: bfloat16 [1024, 8192], P(None, 'row'), may hold values from -6 to 6
- positions: int32 [512], replicated, may hold values from 0 to 1023, as said below
- gate_weight: bfloat16 [8192, 28672], P('row', 'col'), may hold values from -0.0625 to 0.0625
- up_weight: bfloat16 [8192, 28672], P('row', 'col'), may hold values from -0.0625 to 0.0625
- inv_cov: bfloat16 [28672, 28672], P('row', 'col'), as said below
- target_res: bfloat16 [8192, 512], P('col'), may hold values from -6080 to 6080
Outputs:
- update: bfloat16 [8192, 28672], P('col', 'row')
The draws below stay inside these ranges and needn't reach their ends.
Inputs may be any that keep to these rules, and one draw needn't show every extreme that they name: The positions of the facts are distinct. inv_cov is symmetric and positive definite.
All inputs are finite; a program needn't handle non-finite values.
Results may differ from the reference program's by a relative error of at most 0.0066.
Values may be sent and summed in bfloat16 or wider, within the bound.
A program may use at most 128 MiB of HBM per device.

```python
import math
import jax
import jax.numpy as jnp
from jax import lax

D = 8192
FF = 28672
FACTS = 512
TOKENS = 1024


def draw_inv_cov(key, part):
    key_off = jax.random.fold_in(key, 11)
    key_diag = jax.random.fold_in(key, 12)
    diag_base = 12.0 / FF
    spread = diag_base / (5.0 * math.sqrt(FF))
    noise_full = jax.random.normal(key_off, (FF, FF), jnp.float32)
    diagonal = diag_base * jax.random.uniform(key_diag, (FF,), jnp.float32, 0.7, 1.6)
    symmetric = (noise_full + noise_full.T) * (spread / math.sqrt(2.0))
    diag_index = jnp.arange(FF)
    return symmetric.at[diag_index, diag_index].add(diagonal).astype(jnp.bfloat16)


def draw_positions(key, part):
    interior = jax.random.permutation(jax.random.fold_in(key, 21), TOKENS - 2)[:FACTS - 2] + 1
    end_points = jnp.array([0, TOKENS - 1], jnp.int32)
    chosen = jnp.concatenate([interior.astype(jnp.int32), end_points])
    ordering = jax.random.permutation(jax.random.fold_in(key, 22), FACTS)
    return chosen[ordering]


def levels(rng, extent, shards, least, largest):
    def one(position, blocks):
        draws = jax.random.uniform(jax.random.fold_in(jax.random.fold_in(rng, 6), position), (blocks,), jnp.float32, least / len(shards), largest / len(shards))
        return jnp.repeat(jnp.exp(draws), extent[position] // blocks).reshape((-1,) + (1,) * (len(extent) - position - 1))

    level = one(*shards[0])
    for cut in shards[1:]:
        level = level * one(*cut)
    return level


def gaussian(rng, extent, width, reach, split=(), kind=jnp.bfloat16):
    values = jax.random.normal(rng, extent, jnp.float32) * width
    if len(split) > 0:
        values = levels(rng, extent, split, -0.22, 0.18) * values
    return jnp.clip(values, min=-reach, max=reach).astype(kind)


def setup_inputs(seed: int = 0) -> dict:
    arg_keys = jax.random.split(jax.random.key(seed), 7)
    hidden = gaussian(arg_keys[0], (TOKENS, D), 1.0, 6.0, ((1, 16),))
    positions = draw_positions(jax.random.fold_in(arg_keys[6], 71), 0)
    gate_weight = gaussian(arg_keys[2], (D, FF), D ** -0.5, 0.0625, ((0, 16), (1, 16)))
    up_weight = gaussian(arg_keys[3], (D, FF), D ** -0.5, 0.0625, ((0, 16), (1, 16)))
    inv_cov = draw_inv_cov(jax.random.fold_in(arg_keys[6], 71), 0)
    target_res = gaussian(arg_keys[5], (D, FACTS), (0.8 * FF * FACTS ** -0.5), 6080.0, ((0, 16),))
    return dict(hidden=hidden, positions=positions, gate_weight=gate_weight, up_weight=up_weight, inv_cov=inv_cov, target_res=target_res)


def right_solve(system, target):
    factor = jnp.linalg.cholesky(system)
    halfway = lax.linalg.triangular_solve(factor, target, left_side=False, lower=True, transpose_a=True)
    return lax.linalg.triangular_solve(factor, halfway, left_side=False, lower=True, transpose_a=False)

def reference(hidden, positions, gate_weight, up_weight, inv_cov, target_res):
    subject = jnp.take(hidden, positions.astype(jnp.int32), axis=0)
    gate_out = jnp.dot(subject.astype(jnp.float32), gate_weight.astype(jnp.float32), preferred_element_type=jnp.float32)
    up_out = jnp.dot(subject.astype(jnp.float32), up_weight.astype(jnp.float32), preferred_element_type=jnp.float32)
    keys = (jax.nn.silu(gate_out) * up_out).astype(jnp.bfloat16)
    image = jnp.dot(keys.astype(jnp.float32), inv_cov.astype(jnp.float32), preferred_element_type=jnp.float32)
    keys_wide = keys.astype(jnp.float32)
    identity = jnp.eye(keys.shape[0], dtype=jnp.float32)
    system = identity + lax.dot_general(keys_wide, image, (((1,), (1,)), ((), ())), precision=lax.Precision.HIGHEST)
    coeffs = right_solve(system, target_res.astype(jnp.float32)).astype(jnp.bfloat16)
    image_short = image.astype(jnp.bfloat16)
    return jnp.dot(coeffs.astype(jnp.float32), image_short.astype(jnp.float32), preferred_element_type=jnp.float32).astype(jnp.bfloat16)
```

```python
import jax
import jax.numpy as jnp
from jax import lax
from jax.experimental import pallas as pl
from jax.experimental.pallas import tpu as pltpu
from jax.sharding import PartitionSpec as P

MESH = pl.DeviceIdType.MESH
F32 = jnp.float32
BF16 = jnp.bfloat16


def exchange_kernel(
    gu, cov_hbm, s_out, img_out,
    cov, ysend, yrecv, psend, precv, plast_s, plast_r,
    qsend, qrecv, qlast_s, qlast_r, qy_s, qy_r,
    kt, kts, cxs, cxr, cs, cr, spart, exs, exr, e1s, e1r, e2s, e2r, e3, s2,
    cov_sem, y_ss, y_rs, z_ss, z_rs, qy_ss, qy_rs, b_ss, b_rs, t_ss, t_rs,
    cx_ss, cx_rs, c_ss, c_rs, ex_ss, ex_rs, e1_ss, e1_rs, e2_ss, e2_rs,
    e3_ss, e3_rs, e4_ss, e4_rs, d_ss, d_rs, loc_sem,
):
    ch = kt.shape[0] // 16
    half = kt.shape[1] // 2
    me_r, me_c = lax.axis_index("row"), lax.axis_index("col")
    y, z = me_r // 8, me_r % 8
    g, core = me_c // 2, me_c % 2

    def send(src, dst, ss, rs, r, c):
        return pltpu.make_async_remote_copy(
            src_ref=src, dst_ref=dst, send_sem=ss, recv_sem=rs,
            device_id=(r, c), device_id_type=MESH,
        )

    def rows(i, n=ch):
        return pl.ds(pl.multiple_of(i * n, 8), n)

    y_to = ((1 - y) * 8 + z, me_c)

    def z_to(step):
        return (y * 8 + (z + step + 8) % 8, me_c)

    partner = (me_r, g * 2 + 1 - core)

    def g_to(k):
        return (me_r, ((g + k) % 8) * 2 + core)

    own_sub = core * 8 + (g + 4) % 8
    t_out = (me_c, ((me_r % 8 + 4) % 8) * 2 + me_r // 8)
    t_in = (own_sub, me_r)

    cov_copy = pltpu.make_async_copy(cov_hbm, cov, cov_sem)
    cov_copy.start()
    kts[...] = jnp.zeros_like(kts)

    barrier = pltpu.get_barrier_semaphore()
    peers = [((me_r + k) % 16, me_c) for k in range(1, 16)]
    peers += [g_to(k) for k in range(1, 8)] + [partner, t_out, t_in]
    for p in peers:
        pl.semaphore_signal(barrier, inc=1, device_id=p, device_id_type=MESH)
    pl.semaphore_wait(barrier, len(peers))

    lo, hi = pl.ds(0, half), pl.ds(half, half)
    pending = []

    ycopies = {}
    for o in (4, 3, 5, 2, 6, 1, 7, 0):
        ysend[o] = gu[:, rows((1 - y) * 8 + (z + o) % 8), lo].astype(BF16)
        ycopies[o] = send(ysend.at[o], yrecv.at[o], y_ss.at[o], y_rs.at[o], *y_to)
        ycopies[o].start()

    def p_own(o):
        return gu[:, rows(y * 8 + (z + o) % 8), lo] + yrecv[o].astype(F32)

    def q_own(o, yy):
        return gu[:, rows(yy * 8 + (z + o) % 8), hi]

    copies = {}
    for s in range(1, 5):
        for side in (0, 1):
            if side == 1 and s == 1:
                continue
            last = s == 4
            slot = side * 3 + s - 1 - side
            sign = -1 if side == 0 else 1
            o = (sign * (5 - s)) % 8
            first = s == 1 + side
            if not first:
                copies["q", side, s - 1].wait_recv()
            for yy in (0, 1):
                v = q_own(o, yy)
                if not first:
                    v = v + qrecv[slot - 1, yy].astype(F32)
                if last:
                    qlast_s[side, yy] = v
                else:
                    qsend[slot, yy] = v.astype(BF16)
            if last:
                src, dst = qlast_s.at[side], qlast_r.at[side]
            else:
                src, dst = qsend.at[slot], qrecv.at[slot]
            i = side * 4 + s - 1
            cp = send(src, dst, z_ss.at[i], z_rs.at[i], *z_to(sign))
            cp.start()
            copies["q", side, s] = cp
            sign = -sign
            o = (sign * (5 - s)) % 8
            ycopies[o].wait_recv()
            v = p_own(o)
            if not first:
                copies["p", side, s - 1].wait_recv()
                v = v + precv[slot - 1].astype(F32)
            if last:
                plast_s[side] = v
                src, dst = plast_s.at[side], plast_r.at[side]
            else:
                psend[slot] = v.astype(BF16)
                src, dst = psend.at[slot], precv.at[slot]
            i = 8 + side * 4 + s - 1
            cp = send(src, dst, z_ss.at[i], z_rs.at[i], *z_to(sign))
            cp.start()
            copies["p", side, s] = cp
    copies["q", 0, 4].wait_recv()
    copies["q", 1, 4].wait_recv()
    qy_s[...] = q_own(0, 1 - y) + qlast_r[0, 1 - y] + qlast_r[1, 1 - y]
    qy = send(qy_s, qy_r, qy_ss, qy_rs, *y_to)
    qy.start()
    ycopies[0].wait_recv()
    copies["p", 0, 4].wait_recv()
    copies["p", 1, 4].wait_recv()
    v = p_own(0) + plast_r[0] + plast_r[1]
    kt[rows(me_r), lo] = (v[0] / (1.0 + jnp.exp(-v[0])) * v[1]).astype(BF16)
    qy.wait_recv()
    v = q_own(0, y) + qlast_r[0, y] + qlast_r[1, y] + qy_r[...]
    kt[rows(me_r), hi] = (v[0] / (1.0 + jnp.exp(-v[0])) * v[1]).astype(BF16)
    pending += list(ycopies.values()) + list(copies.values()) + [qy]

    def shard(zo, rel):
        yy = y if rel == 0 else 1 - y
        return rows(yy * 8 + (zo + 8) % 8)

    mine = kt.at[rows(me_r)]
    b_y = send(mine, mine, b_ss.at[32], b_rs.at[32], *y_to)
    b_y.start()
    bc = {}

    def forward(h, side, t, rel):
        sign = 1 if h == side else -1
        ref = kt.at[shard(z - sign * (t - 1), rel), lo if h == 0 else hi]
        i = h * 16 + side * 8 + (t - 1) * 2 + rel
        cp = send(ref, ref, b_ss.at[i], b_rs.at[i], *z_to(sign))
        cp.start()
        bc[h, side, t, rel] = cp

    for side in (0, 1):
        for h in (0, 1):
            forward(h, side, 1, 0)
    tr = send(mine, kts.at[pl.ds(0, ch)], t_ss, t_rs, *t_out)
    tr.start()
    b_y.wait_recv()
    for side in (0, 1):
        for h in (0, 1):
            forward(h, side, 1, 1)
    for t in range(2, 5):
        for rel in (0, 1):
            for side in (0, 1):
                for h in (0, 1):
                    if side == 1 and t == 4:
                        continue
                    bc[h, side, t - 1, rel].wait_recv()
                    forward(h, side, t, rel)
    for rel in (0, 1):
        for h in (0, 1):
            bc[h, 1, 3, rel].wait_recv()
            bc[h, 0, 4, rel].wait_recv()
    pending += [b_y, tr] + list(bc.values())

    cov_copy.wait()

    def product(sub):
        return jnp.dot(cov[rows(sub), :], kt[...], preferred_element_type=F32)

    def sub_of(k, cc):
        return cc * 8 + (g + k + 4) % 8

    def cx_copy(k):
        return send(cxs.at[k], cxr.at[k], cx_ss.at[k], cx_rs.at[k], *partner)

    def c_copy(k):
        return send(cs.at[k], cr.at[k], c_ss.at[k], c_rs.at[k], *g_to(k))

    def far(k, carry):
        kk = (k + 1) % 8
        cxs[kk] = product(sub_of(kk, 1 - core)).astype(BF16)
        cx_copy(kk).start()
        return carry

    lax.fori_loop(0, 8, far, 0)

    def near(k, carry):
        v = product(sub_of(k, core))
        cx_copy(k).wait_recv()
        cs[k] = (v + cxr[k].astype(F32)).astype(BF16)
        c_copy(k).start()
        return carry

    lax.fori_loop(1, 8, near, 0)
    v = product(sub_of(0, core))
    cx_copy(0).wait_recv()
    v = v + cxr[0].astype(F32)
    for k in range(1, 8):
        c_copy(k).wait_recv()
        v = v + cr[k].astype(F32)
    v_hi = v.astype(BF16)
    v_lo = (v - v_hi.astype(F32)).astype(BF16)
    img_out[rows(own_sub), :] = v_hi

    tr.wait_recv()
    pad = jnp.zeros((kts.shape[0] - ch, kts.shape[1]), BF16)
    dims = (((0,), (0,)), ((), ()))
    keys_s = kts[...]
    part = lax.dot_general(
        keys_s, jnp.concatenate([v_hi, pad], 0), dims, preferred_element_type=F32
    ) + lax.dot_general(
        keys_s, jnp.concatenate([v_lo, pad], 0), dims, preferred_element_type=F32
    )
    spart[...] = part
    n2 = spart.shape[0] // 2
    exs[...] = spart[rows(1 - core, n2), :].astype(BF16)
    ex = send(exs, exr, ex_ss, ex_rs, *partner)
    ex.start()
    ex.wait_recv()
    e1s[...] = (spart[rows(core, n2), :] + exr[...].astype(F32))
    blk = n2 // 8
    e1c = []
    for k in range(1, 8):
        e2s[k] = e1s[rows((g + k) % 8, blk), :].astype(BF16)
        cp = send(e2s.at[k], e1r.at[k], e1_ss.at[k], e1_rs.at[k], *g_to(k))
        cp.start()
        e1c.append(cp)
    dc = {}
    mine = img_out.at[rows(own_sub)]

    def gather(ref_of, ss, rs, out):
        for k in range(1, 8):
            ref = ref_of(g)
            out[k] = send(ref, ref, ss.at[k], rs.at[k], *g_to(k))
            out[k].start()
        ref = ref_of(g)
        out[0] = send(ref, ref, ss.at[0], rs.at[0], *partner)
        out[0].start()

    def relay(ref_of, ss, rs, out):
        for k in range(1, 8):
            out[k].wait_recv()
            ref = ref_of((g - k + 8) % 8)
            out[7 + k] = send(ref, ref, ss.at[7 + k], rs.at[7 + k], *partner)
            out[7 + k].start()

    def img_ref(gg):
        return img_out.at[rows(core * 8 + (gg + 4) % 8)]

    def s_ref(gg):
        return s_out.at[rows(core * 8 + gg, blk)]

    gather(img_ref, d_ss, d_rs, dc)
    v = e1s[rows(g, blk), :]
    for k in range(1, 8):
        e1c[k - 1].wait_recv()
        v = v + e1r[k].astype(F32)
    s2[...] = v
    e1s[pl.ds(0, blk), :] = v
    tile = pl.ds(0, blk)

    def piece(ref, i):
        return ref.at[rows(i // 4, 8), pl.ds(pl.multiple_of(i % 4 * 128, 128), 128)]

    e2c = []
    for k in range(1, 16):
        cp = send(
            piece(e1s, (me_r + k) % 16), e2r.at[k], e2_ss.at[k], e2_rs.at[k],
            (me_r + k) % 16, me_c,
        )
        cp.start()
        e2c.append(cp)
    at_rows = rows(me_r // 4, 8)
    at_cols = pl.ds(pl.multiple_of(me_r % 4 * 128, 128), 128)
    v = e1s[at_rows, at_cols]
    for k in range(1, 16):
        e2c[k - 1].wait_recv()
        v = v + e2r[k]
    e3[...] = v
    e3c = []
    for k in range(1, 16):
        cp = send(
            e3, s2.at[at_rows, at_cols], e3_ss.at[k], e3_rs.at[k],
            (me_r + k) % 16, me_c,
        )
        cp.start()
        e3c.append(cp)
    s2[at_rows, at_cols] = v
    for cp in e3c:
        cp.wait_recv()
    s_out[rows(core * 8 + g, blk), :] = s2[...]
    ec = {}
    gather(s_ref, e4_ss, e4_rs, ec)
    relay(s_ref, e4_ss, e4_rs, ec)
    relay(img_ref, d_ss, d_rs, dc)
    for out in (ec, dc):
        out[0].wait_recv()
        for k in range(1, 8):
            out[7 + k].wait_recv()
    pending += [ex] + e1c + e2c + e3c + list(ec.values()) + list(dc.values())
    for cp in pending:
        cp.wait_send()
    for k in range(8):
        cx_copy(k).wait_send()
    for k in range(1, 8):
        c_copy(k).wait_send()


def exchange(gu, inv_cov):
    ff, facts = gu.shape[1:]
    ch, half, blk = ff // 16, facts // 2, facts // 16
    dma = pltpu.SemaphoreType.DMA
    vm = pltpu.VMEM
    scratch = [
        vm(inv_cov.shape, BF16),
        vm((8, 2, ch, half), BF16), vm((8, 2, ch, half), BF16),
        vm((5, 2, ch, half), BF16), vm((5, 2, ch, half), BF16),
        vm((2, 2, ch, half), F32), vm((2, 2, ch, half), F32),
        vm((5, 2, 2, ch, half), BF16), vm((5, 2, 2, ch, half), BF16),
        vm((2, 2, 2, ch, half), F32), vm((2, 2, 2, ch, half), F32),
        vm((2, ch, half), F32), vm((2, ch, half), F32),
        vm((ff, facts), BF16), vm((-(-ch // 128) * 128, facts), BF16),
        vm((8, ch, facts), BF16), vm((8, ch, facts), BF16),
        vm((8, ch, facts), BF16), vm((8, ch, facts), BF16),
        vm((facts, facts), F32),
        vm((facts // 2, facts), BF16), vm((facts // 2, facts), BF16),
        vm((facts // 2, facts), F32), vm((8, blk, facts), BF16),
        vm((8, blk, facts), BF16), vm((16, 8, 128), F32), vm((8, 128), F32),
        vm((blk, facts), F32),
        dma(()), dma((8,)), dma((8,)), dma((16,)), dma((16,)), dma(()), dma(()),
        dma((33,)), dma((33,)), dma(()), dma(()),
        dma((8,)), dma((8,)), dma((8,)), dma((8,)), dma(()), dma(()),
        dma((8,)), dma((8,)), dma((16,)), dma((16,)), dma((16,)), dma((16,)),
        dma((15,)), dma((15,)), dma((15,)), dma((15,)), dma(()),
    ]
    return pl.pallas_call(
        exchange_kernel,
        name="exchange",
        out_shape=(
            jax.ShapeDtypeStruct((facts, facts), F32),
            jax.ShapeDtypeStruct((ff, facts), BF16),
        ),
        in_specs=[
            pl.BlockSpec(memory_space=pltpu.VMEM),
            pl.BlockSpec(memory_space=pl.ANY),
        ],
        out_specs=[pl.BlockSpec(memory_space=pltpu.VMEM)] * 2,
        scratch_shapes=scratch,
        compiler_params=pltpu.CompilerParams(
            collective_id=0, has_side_effects=True, vmem_limit_bytes=60 * 2**20
        ),
    )(gu, inv_cov)


def right_solve(system, target):
    factor = jnp.linalg.cholesky(system)
    halfway = lax.linalg.triangular_solve(
        factor, target, left_side=False, lower=True, transpose_a=True
    )
    return lax.linalg.triangular_solve(
        factor, halfway, left_side=False, lower=True, transpose_a=False
    )


def per_device(hidden, positions, gate_weight, up_weight, inv_cov, target_res):
    facts = positions.shape[0]
    subject = jnp.take(hidden, positions, axis=0)
    dims = (((0,), (1,)), ((), ()))
    gate = lax.dot_general(gate_weight, subject, dims, preferred_element_type=F32)
    up = lax.dot_general(up_weight, subject, dims, preferred_element_type=F32)
    system, image_t = exchange(jnp.stack([gate, up]), inv_cov)
    system = system + jnp.eye(facts, dtype=F32)
    coeffs = right_solve(system, target_res.astype(F32)).astype(BF16)
    return lax.dot_general(
        coeffs, image_t, (((1,), (1,)), ((), ())), preferred_element_type=F32
    ).astype(BF16)


def solution(mesh):
    return jax.shard_map(
        per_device,
        mesh=mesh,
        in_specs=(
            P(None, "row"),
            P(),
            P("row", "col"),
            P("row", "col"),
            P("row", "col"),
            P("col", None),
        ),
        out_specs=P("col", "row"),
        check_vma=False,
    )
```

```python
import jax
import jax.numpy as jnp
from jax import lax
from jax.experimental import pallas as pl
from jax.experimental.pallas import tpu as pltpu
from jax.sharding import PartitionSpec as P

MESH = pl.DeviceIdType.MESH
F32 = jnp.float32
BF16 = jnp.bfloat16


def exchange_kernel(
    gu, cov_hbm, s_out, img_out,
    cov, ysend, yrecv, psend, precv, plast_s, plast_r,
    qsend, qrecv, qlast_s, qlast_r, qy_s, qy_r,
    kt, kts, cxs, cxr, cs, cr, spart, exs, exr, e1s, e1r, e2s, e2r, e3, s2,
    cov_sem, y_ss, y_rs, z_ss, z_rs, qy_ss, qy_rs, b_ss, b_rs, t_ss, t_rs,
    cx_ss, cx_rs, c_ss, c_rs, ex_ss, ex_rs, e1_ss, e1_rs, e2_ss, e2_rs,
    e3_ss, e3_rs, e4_ss, e4_rs, d_ss, d_rs, loc_sem,
):
    ch = kt.shape[0] // 16
    half = kt.shape[1] // 2
    me_r, me_c = lax.axis_index("row"), lax.axis_index("col")
    y, z = me_r // 8, me_r % 8
    g, core = me_c // 2, me_c % 2

    def send(src, dst, ss, rs, r, c):
        return pltpu.make_async_remote_copy(
            src_ref=src, dst_ref=dst, send_sem=ss, recv_sem=rs,
            device_id=(r, c), device_id_type=MESH,
        )

    def rows(i, n=ch):
        return pl.ds(pl.multiple_of(i * n, 8), n)

    y_to = ((1 - y) * 8 + z, me_c)

    def z_to(step):
        return (y * 8 + (z + step + 8) % 8, me_c)

    partner = (me_r, g * 2 + 1 - core)

    def g_to(k):
        return (me_r, ((g + k) % 8) * 2 + core)

    own_sub = core * 8 + (g + 4) % 8
    t_out = (me_c, ((me_r % 8 + 4) % 8) * 2 + me_r // 8)
    t_in = (own_sub, me_r)

    cov_copy = pltpu.make_async_copy(cov_hbm, cov, cov_sem)
    cov_copy.start()
    kts[...] = jnp.zeros_like(kts)

    barrier = pltpu.get_barrier_semaphore()
    peers = [((me_r + k) % 16, me_c) for k in range(1, 16)]
    peers += [g_to(k) for k in range(1, 8)] + [partner, t_out, t_in]
    for p in peers:
        pl.semaphore_signal(barrier, inc=1, device_id=p, device_id_type=MESH)
    pl.semaphore_wait(barrier, len(peers))

    lo, hi = pl.ds(0, half), pl.ds(half, half)
    pending = []

    ycopies = {}
    for o in (4, 3, 5, 2, 6, 1, 7, 0):
        ysend[o] = gu[:, rows((1 - y) * 8 + (z + o) % 8), lo].astype(BF16)
        ycopies[o] = send(ysend.at[o], yrecv.at[o], y_ss.at[o], y_rs.at[o], *y_to)
        ycopies[o].start()

    def p_own(o):
        return gu[:, rows(y * 8 + (z + o) % 8), lo] + yrecv[o].astype(F32)

    def q_own(o, yy):
        return gu[:, rows(yy * 8 + (z + o) % 8), hi]

    copies = {}
    for s in range(1, 5):
        for side in (0, 1):
            if side == 1 and s == 1:
                continue
            last = s == 4
            slot = side * 3 + s - 1 - side
            sign = -1 if side == 0 else 1
            o = (sign * (5 - s)) % 8
            first = s == 1 + side
            if not first:
                copies["q", side, s - 1].wait_recv()
            for yy in (0, 1):
                v = q_own(o, yy)
                if not first:
                    v = v + qrecv[slot - 1, yy].astype(F32)
                if last:
                    qlast_s[side, yy] = v
                else:
                    qsend[slot, yy] = v.astype(BF16)
            if last:
                src, dst = qlast_s.at[side], qlast_r.at[side]
            else:
                src, dst = qsend.at[slot], qrecv.at[slot]
            i = side * 4 + s - 1
            cp = send(src, dst, z_ss.at[i], z_rs.at[i], *z_to(sign))
            cp.start()
            copies["q", side, s] = cp
            sign = -sign
            o = (sign * (5 - s)) % 8
            ycopies[o].wait_recv()
            v = p_own(o)
            if not first:
                copies["p", side, s - 1].wait_recv()
                v = v + precv[slot - 1].astype(F32)
            if last:
                plast_s[side] = v
                src, dst = plast_s.at[side], plast_r.at[side]
            else:
                psend[slot] = v.astype(BF16)
                src, dst = psend.at[slot], precv.at[slot]
            i = 8 + side * 4 + s - 1
            cp = send(src, dst, z_ss.at[i], z_rs.at[i], *z_to(sign))
            cp.start()
            copies["p", side, s] = cp
    copies["q", 0, 4].wait_recv()
    copies["q", 1, 4].wait_recv()
    qy_s[...] = q_own(0, 1 - y) + qlast_r[0, 1 - y] + qlast_r[1, 1 - y]
    qy = send(qy_s, qy_r, qy_ss, qy_rs, *y_to)
    qy.start()
    ycopies[0].wait_recv()
    copies["p", 0, 4].wait_recv()
    copies["p", 1, 4].wait_recv()
    v = p_own(0) + plast_r[0] + plast_r[1]
    kt[rows(me_r), lo] = (v[0] / (1.0 + jnp.exp(-v[0])) * v[1]).astype(BF16)
    qy.wait_recv()
    v = q_own(0, y) + qlast_r[0, y] + qlast_r[1, y] + qy_r[...]
    kt[rows(me_r), hi] = (v[0] / (1.0 + jnp.exp(-v[0])) * v[1]).astype(BF16)
    pending += list(ycopies.values()) + list(copies.values()) + [qy]

    def shard(zo, rel):
        yy = y if rel == 0 else 1 - y
        return rows(yy * 8 + (zo + 8) % 8)

    mine = kt.at[rows(me_r)]
    b_y = send(mine, mine, b_ss.at[32], b_rs.at[32], *y_to)
    b_y.start()
    bc = {}

    def forward(h, side, t, rel):
        sign = 1 if h == side else -1
        ref = kt.at[shard(z - sign * (t - 1), rel), lo if h == 0 else hi]
        i = h * 16 + side * 8 + (t - 1) * 2 + rel
        cp = send(ref, ref, b_ss.at[i], b_rs.at[i], *z_to(sign))
        cp.start()
        bc[h, side, t, rel] = cp

    for side in (0, 1):
        for h in (0, 1):
            forward(h, side, 1, 0)
    tr = send(mine, kts.at[pl.ds(0, ch)], t_ss, t_rs, *t_out)
    tr.start()
    b_y.wait_recv()
    for side in (0, 1):
        for h in (0, 1):
            forward(h, side, 1, 1)
    for t in range(2, 5):
        for rel in (0, 1):
            for side in (0, 1):
                for h in (0, 1):
                    if side == 1 and t == 4:
                        continue
                    bc[h, side, t - 1, rel].wait_recv()
                    forward(h, side, t, rel)
    for rel in (0, 1):
        for h in (0, 1):
            bc[h, 1, 3, rel].wait_recv()
            bc[h, 0, 4, rel].wait_recv()
    pending += [b_y, tr] + list(bc.values())

    cov_copy.wait()

    def product(sub):
        return jnp.dot(cov[rows(sub), :], kt[...], preferred_element_type=F32)

    def sub_of(k, cc):
        return cc * 8 + (g + k + 4) % 8

    def cx_copy(k):
        return send(cxs.at[k], cxr.at[k], cx_ss.at[k], cx_rs.at[k], *partner)

    def c_copy(k):
        return send(cs.at[k], cr.at[k], c_ss.at[k], c_rs.at[k], *g_to(k))

    def far(k, carry):
        kk = (k + 1) % 8
        cxs[kk] = product(sub_of(kk, 1 - core)).astype(BF16)
        cx_copy(kk).start()
        return carry

    lax.fori_loop(0, 8, far, 0)

    def near(k, carry):
        v = product(sub_of(k, core))
        cx_copy(k).wait_recv()
        cs[k] = (v + cxr[k].astype(F32)).astype(BF16)
        c_copy(k).start()
        return carry

    lax.fori_loop(1, 8, near, 0)
    v = product(sub_of(0, core))
    cx_copy(0).wait_recv()
    v = v + cxr[0].astype(F32)
    for k in range(1, 8):
        c_copy(k).wait_recv()
        v = v + cr[k].astype(F32)
    v_hi = v.astype(BF16)
    v_lo = (v - v_hi.astype(F32)).astype(BF16)
    img_out[rows(own_sub), :] = v_hi

    tr.wait_recv()
    pad = jnp.zeros((kts.shape[0] - ch, kts.shape[1]), BF16)
    dims = (((0,), (0,)), ((), ()))
    keys_s = kts[...]
    part = lax.dot_general(
        keys_s, jnp.concatenate([v_hi, pad], 0), dims, preferred_element_type=F32
    ) + lax.dot_general(
        keys_s, jnp.concatenate([v_lo, pad], 0), dims, preferred_element_type=F32
    )
    spart[...] = part
    n2 = spart.shape[0] // 2
    exs[...] = spart[rows(1 - core, n2), :].astype(BF16)
    ex = send(exs, exr, ex_ss, ex_rs, *partner)
    ex.start()
    ex.wait_recv()
    e1s[...] = (spart[rows(core, n2), :] + exr[...].astype(F32))
    blk = n2 // 8
    e1c = []
    for k in range(1, 8):
        e2s[k] = e1s[rows((g + k) % 8, blk), :].astype(BF16)
        cp = send(e2s.at[k], e1r.at[k], e1_ss.at[k], e1_rs.at[k], *g_to(k))
        cp.start()
        e1c.append(cp)
    dc = {}
    mine = img_out.at[rows(own_sub)]

    def gather(ref_of, ss, rs, out):
        for k in range(1, 8):
            ref = ref_of(g)
            out[k] = send(ref, ref, ss.at[k], rs.at[k], *g_to(k))
            out[k].start()
        ref = ref_of(g)
        out[0] = send(ref, ref, ss.at[0], rs.at[0], *partner)
        out[0].start()

    def relay(ref_of, ss, rs, out):
        for k in range(1, 8):
            out[k].wait_recv()
            ref = ref_of((g - k + 8) % 8)
            out[7 + k] = send(ref, ref, ss.at[7 + k], rs.at[7 + k], *partner)
            out[7 + k].start()

    def img_ref(gg):
        return img_out.at[rows(core * 8 + (gg + 4) % 8)]

    def s_ref(gg):
        return s_out.at[rows(core * 8 + gg, blk)]

    gather(img_ref, d_ss, d_rs, dc)
    v = e1s[rows(g, blk), :]
    for k in range(1, 8):
        e1c[k - 1].wait_recv()
        v = v + e1r[k].astype(F32)
    s2[...] = v
    e1s[pl.ds(0, blk), :] = v
    tile = pl.ds(0, blk)

    def piece(ref, i):
        return ref.at[rows(i // 4, 8), pl.ds(pl.multiple_of(i % 4 * 128, 128), 128)]

    e2c = []
    for k in range(1, 16):
        cp = send(
            piece(e1s, (me_r + k) % 16), e2r.at[k], e2_ss.at[k], e2_rs.at[k],
            (me_r + k) % 16, me_c,
        )
        cp.start()
        e2c.append(cp)
    at_rows = rows(me_r // 4, 8)
    at_cols = pl.ds(pl.multiple_of(me_r % 4 * 128, 128), 128)
    v = e1s[at_rows, at_cols]
    for k in range(1, 16):
        e2c[k - 1].wait_recv()
        v = v + e2r[k]
    e3[...] = v
    e3c = []
    for k in range(1, 16):
        cp = send(
            e3, s2.at[at_rows, at_cols], e3_ss.at[k], e3_rs.at[k],
            (me_r + k) % 16, me_c,
        )
        cp.start()
        e3c.append(cp)
    s2[at_rows, at_cols] = v
    for cp in e3c:
        cp.wait_recv()
    s_out[rows(core * 8 + g, blk), :] = s2[...]
    ec = {}
    gather(s_ref, e4_ss, e4_rs, ec)
    relay(s_ref, e4_ss, e4_rs, ec)
    relay(img_ref, d_ss, d_rs, dc)
    for out in (ec, dc):
        out[0].wait_recv()
        for k in range(1, 8):
            out[7 + k].wait_recv()
    pending += [ex] + e1c + e2c + e3c + list(ec.values()) + list(dc.values())
    for cp in pending:
        cp.wait_send()
    for k in range(8):
        cx_copy(k).wait_send()
    for k in range(1, 8):
        c_copy(k).wait_send()


def exchange(gu, inv_cov):
    ff, facts = gu.shape[1:]
    ch, half, blk = ff // 16, facts // 2, facts // 16
    dma = pltpu.SemaphoreType.DMA
    vm = pltpu.VMEM
    scratch = [
        vm(inv_cov.shape, BF16),
        vm((8, 2, ch, half), BF16), vm((8, 2, ch, half), BF16),
        vm((5, 2, ch, half), BF16), vm((5, 2, ch, half), BF16),
        vm((2, 2, ch, half), F32), vm((2, 2, ch, half), F32),
        vm((5, 2, 2, ch, half), BF16), vm((5, 2, 2, ch, half), BF16),
        vm((2, 2, 2, ch, half), F32), vm((2, 2, 2, ch, half), F32),
        vm((2, ch, half), F32), vm((2, ch, half), F32),
        vm((ff, facts), BF16), vm((-(-ch // 128) * 128, facts), BF16),
        vm((8, ch, facts), BF16), vm((8, ch, facts), BF16),
        vm((8, ch, facts), BF16), vm((8, ch, facts), BF16),
        vm((facts, facts), F32),
        vm((facts // 2, facts), BF16), vm((facts // 2, facts), BF16),
        vm((facts // 2, facts), F32), vm((8, blk, facts), BF16),
        vm((8, blk, facts), BF16), vm((16, 8, 128), F32), vm((8, 128), F32),
        vm((blk, facts), F32),
        dma(()), dma((8,)), dma((8,)), dma((16,)), dma((16,)), dma(()), dma(()),
        dma((33,)), dma((33,)), dma(()), dma(()),
        dma((8,)), dma((8,)), dma((8,)), dma((8,)), dma(()), dma(()),
        dma((8,)), dma((8,)), dma((16,)), dma((16,)), dma((16,)), dma((16,)),
        dma((15,)), dma((15,)), dma((15,)), dma((15,)), dma(()),
    ]
    return pl.pallas_call(
        exchange_kernel,
        name="exchange",
        out_shape=(
            jax.ShapeDtypeStruct((facts, facts), F32),
            jax.ShapeDtypeStruct((ff, facts), BF16),
        ),
        in_specs=[
            pl.BlockSpec(memory_space=pltpu.VMEM),
            pl.BlockSpec(memory_space=pl.ANY),
        ],
        out_specs=[pl.BlockSpec(memory_space=pltpu.VMEM)] * 2,
        scratch_shapes=scratch,
        compiler_params=pltpu.CompilerParams(
            collective_id=0, has_side_effects=True, vmem_limit_bytes=60 * 2**20
        ),
    )(gu, inv_cov)


def invert(m):
    n = m.shape[0]
    lane = lax.broadcasted_iota(jnp.int32, (1, n), 1)
    sub = lax.broadcasted_iota(jnp.int32, (n, 1), 0)
    for p in range(n):
        row = m[p : p + 1, :]
        col = m[:, p : p + 1]
        r = 1.0 / jnp.broadcast_to(m[p : p + 1, p : p + 1], (1, n))
        row = jnp.where(lane == p, r, row * r)
        m = jnp.where(sub == p, row, jnp.where(lane == p, 0.0, m) - col * row)
    return m


def solve_kernel(s_ref, t_ref, img_ref, out_ref, a):
    n = s_ref.shape[0]
    b = min(128, n)
    eye = lax.broadcasted_iota(jnp.int32, (n, n), 0) == lax.broadcasted_iota(
        jnp.int32, (n, n), 1
    )
    a[...] = s_ref[...] + jnp.where(eye, 1.0, 0.0)

    def dot(p, q):
        return jnp.dot(p, q, precision=lax.Precision.HIGHEST, preferred_element_type=F32)

    def block(k, carry):
        d = pl.ds(pl.multiple_of(k * b, b), b)
        inv = invert(a[d, d])
        col = a[:, d]
        wide = dot(inv, a[d, :])
        a[...] = a[...] - dot(col, wide)
        a[:, d] = -dot(col, inv)
        a[d, :] = wide
        a[d, d] = inv
        return carry

    lax.fori_loop(0, n // b, block, 0)
    v = a[...]
    coeffs = jnp.zeros((t_ref.shape[0], n), F32)
    for _ in range(3):
        short = v.astype(BF16)
        coeffs = coeffs + jnp.dot(t_ref[...], short, preferred_element_type=F32)
        v = v - short.astype(F32)
    coeffs = coeffs.astype(BF16)
    w = 256
    for j in range(out_ref.shape[1] // w):
        out_ref[:, j * w : (j + 1) * w] = lax.dot_general(
            coeffs, img_ref[j * w : (j + 1) * w, :], (((1,), (1,)), ((), ())),
            preferred_element_type=F32,
        ).astype(BF16)


def solve(system, target, image_t):
    n = system.shape[0]
    return pl.pallas_call(
        solve_kernel,
        name="solve",
        out_shape=jax.ShapeDtypeStruct((target.shape[0], image_t.shape[0]), BF16),
        in_specs=[pl.BlockSpec(memory_space=pltpu.VMEM)] * 3,
        out_specs=pl.BlockSpec(memory_space=pltpu.VMEM),
        scratch_shapes=[pltpu.VMEM((n, n), F32)],
        compiler_params=pltpu.CompilerParams(vmem_limit_bytes=40 * 2**20),
    )(system, target, image_t)


def per_device(hidden, positions, gate_weight, up_weight, inv_cov, target_res):
    subject = jnp.take(hidden, positions, axis=0)
    dims = (((0,), (1,)), ((), ()))
    gate = lax.dot_general(gate_weight, subject, dims, preferred_element_type=F32)
    up = lax.dot_general(up_weight, subject, dims, preferred_element_type=F32)
    system, image_t = exchange(jnp.stack([gate, up]), inv_cov)
    return solve(system, target_res, image_t)


def solution(mesh):
    return jax.shard_map(
        per_device,
        mesh=mesh,
        in_specs=(
            P(None, "row"),
            P(),
            P("row", "col"),
            P("row", "col"),
            P("row", "col"),
            P("col", None),
        ),
        out_specs=P("col", "row"),
        check_vma=False,
    )
```

```python
import jax
import jax.numpy as jnp
from jax import lax
from jax.experimental import pallas as pl
from jax.experimental.pallas import tpu as pltpu
from jax.sharding import PartitionSpec as P

MESH = pl.DeviceIdType.MESH
F32 = jnp.float32
BF16 = jnp.bfloat16


def exchange_kernel(
    gate, up, cov_hbm, s_out, img_out,
    cov, ysend, yrecv, psend, precv, qsend, qrecv, qy_s, qy_r,
    kt, kts, cxs, cxr, cs, cr, spart, exs, exr, e1s, e1r, e2s, e2r, e3, s2,
    cov_sem, y_ss, y_rs, z_ss, z_rs, qy_ss, qy_rs, b_ss, b_rs, t_ss, t_rs,
    cx_ss, cx_rs, c_ss, c_rs, ex_ss, ex_rs, e1_ss, e1_rs, e2_ss, e2_rs,
    e3_ss, e3_rs, e4_ss, e4_rs, d_ss, d_rs, loc_sem,
):
    ch = kt.shape[0] // 16
    half = kt.shape[1] // 2
    me_r, me_c = lax.axis_index("row"), lax.axis_index("col")
    y, z = me_r // 8, me_r % 8
    g, core = me_c // 2, me_c % 2

    def send(src, dst, ss, rs, r, c):
        return pltpu.make_async_remote_copy(
            src_ref=src, dst_ref=dst, send_sem=ss, recv_sem=rs,
            device_id=(r, c), device_id_type=MESH,
        )

    def rows(i, n=ch):
        return pl.ds(pl.multiple_of(i * n, 8), n)

    y_to = ((1 - y) * 8 + z, me_c)

    def z_to(step):
        return (y * 8 + (z + step + 8) % 8, me_c)

    partner = (me_r, g * 2 + 1 - core)

    def g_to(k):
        return (me_r, ((g + k) % 8) * 2 + core)

    own_sub = core * 8 + (g + 4) % 8
    t_out = (me_c, ((me_r % 8 + 4) % 8) * 2 + me_r // 8)
    t_in = (own_sub, me_r)

    cov_copy = pltpu.make_async_copy(cov_hbm, cov, cov_sem)
    cov_copy.start()
    kts[...] = jnp.zeros_like(kts)

    barrier = pltpu.get_barrier_semaphore()
    peers = [((me_r + k) % 16, me_c) for k in range(1, 16)]
    peers += [g_to(k) for k in range(1, 8)] + [partner, t_out, t_in]
    for p in peers:
        pl.semaphore_signal(barrier, inc=1, device_id=p, device_id_type=MESH)
    lo, hi = pl.ds(0, half), pl.ds(half, half)
    pending = []

    def projections(r, lanes):
        return jnp.stack([gate[rows(r), lanes], up[rows(r), lanes]])

    order = (4, 3, 5, 2, 6, 1, 7, 0)
    for o in order:
        ysend[o] = projections((1 - y) * 8 + (z + o) % 8, lo).astype(BF16)
    pl.semaphore_wait(barrier, len(peers))
    ycopies = {}
    for o in order:
        ycopies[o] = send(ysend.at[o], yrecv.at[o], y_ss.at[o], y_rs.at[o], *y_to)
        ycopies[o].start()

    def p_own(o):
        return projections(y * 8 + (z + o) % 8, lo) + yrecv[o].astype(F32)

    def q_own(o, yy):
        return projections(yy * 8 + (z + o) % 8, hi)

    copies = {}
    for s in range(1, 5):
        for chain in range(3):
            for side in (0, 1):
                if side == 1 and s == 1:
                    continue
                slot = side * 4 + s - 1 - side
                sign = (-1 if side == 0 else 1) * (-1 if chain == 2 else 1)
                o = (sign * (5 - s)) % 8
                if chain == 2:
                    ycopies[o].wait_recv()
                    v = p_own(o)
                    src, dst = psend.at[slot], precv
                else:
                    v = q_own(o, chain)
                    src, dst = qsend.at[slot, chain], qrecv.at[:, chain]
                if s > 1 + side:
                    copies[chain, side, s - 1].wait_recv()
                    v = v + dst[slot - 1].astype(F32)
                src[...] = v.astype(BF16)
                i = chain * 8 + side * 4 + s - 1
                cp = send(src, dst.at[slot], z_ss.at[i], z_rs.at[i], *z_to(sign))
                cp.start()
                copies[chain, side, s] = cp
    for chain in (0, 1):
        copies[chain, 0, 4].wait_recv()
        copies[chain, 1, 4].wait_recv()

    def q_sum(yy):
        return q_own(0, yy) + qrecv[3, yy].astype(F32) + qrecv[6, yy].astype(F32)

    qy_s[...] = q_sum(1 - y)
    qy = send(qy_s, qy_r, qy_ss, qy_rs, *y_to)
    qy.start()
    ycopies[0].wait_recv()
    copies[2, 0, 4].wait_recv()
    copies[2, 1, 4].wait_recv()
    v = p_own(0) + precv[3].astype(F32) + precv[6].astype(F32)
    kt[rows(me_r), lo] = (v[0] / (1.0 + jnp.exp(-v[0])) * v[1]).astype(BF16)
    v = q_sum(y)
    qy.wait_recv()
    v = v + qy_r[...]
    kt[rows(me_r), hi] = (v[0] / (1.0 + jnp.exp(-v[0])) * v[1]).astype(BF16)
    pending += list(ycopies.values()) + list(copies.values()) + [qy]

    def shard(zo, rel):
        yy = y if rel == 0 else 1 - y
        return rows(yy * 8 + (zo + 8) % 8)

    mine = kt.at[rows(me_r)]
    bc = {}

    def share(ref, i, to, key):
        bc[key] = send(ref, ref, b_ss.at[i], b_rs.at[i], *to)
        bc[key].start()

    def forward(h, side, t, rel):
        sign = 1 if h == side else -1
        ref = kt.at[shard(z - sign * (t - 1), rel), lo if h == 0 else hi]
        share(ref, h * 16 + side * 8 + (t - 1) * 2 + rel, z_to(sign), (h, side, t, rel))

    def across(side, t):
        zo = z + (t if side == 0 else -t)
        share(kt.at[shard(zo, 0), hi], 33 + side * 4 + t, y_to, ("y", side, t))

    share(kt.at[rows(me_r), lo], 32, y_to, "y")
    for side in (0, 1):
        forward(0, side, 1, 0)
        forward(1, side, 1, 0)
    across(0, 0)
    tr = send(mine, kts.at[pl.ds(0, ch)], t_ss, t_rs, *t_out)
    tr.start()
    bc["y"].wait_recv()
    for side in (0, 1):
        forward(0, side, 1, 1)
    for t in range(2, 6):
        for h, rel in ((0, 0), (1, 0), (0, 1)):
            for side in (0, 1):
                if t - 1 > 4 - side:
                    continue
                bc[h, side, t - 1, rel].wait_recv()
                if t <= 4 - side:
                    forward(h, side, t, rel)
                if h == 1:
                    across(side, t - 1)
    for key in list(bc):
        if key != "y" and key[0] == "y":
            bc[key].wait_recv()
    pending += [tr] + list(bc.values())

    cov_copy.wait()

    def product(sub):
        return jnp.dot(cov[rows(sub), :], kt[...], preferred_element_type=F32)

    def sub_of(k, cc):
        return cc * 8 + (g + k + 4) % 8

    def cx_copy(k):
        return send(cxs.at[k], cxr.at[k], cx_ss.at[k], cx_rs.at[k], *partner)

    def c_copy(k):
        return send(cs.at[k], cr.at[k], c_ss.at[k], c_rs.at[k], *g_to(k))

    def far(k):
        cxs[k] = product(sub_of(k, 1 - core)).astype(BF16)
        cx_copy(k).start()

    def near(k):
        v = product(sub_of(k, core))
        cx_copy(k).wait_recv()
        cs[k] = (v + cxr[k].astype(F32)).astype(BF16)
        c_copy(k).start()

    def step(k, carry):
        far((k + 3) % 8)
        near(k + 1)
        return carry

    far(1)
    far(2)
    lax.fori_loop(0, 6, step, 0)
    near(7)
    v = product(sub_of(0, core))
    cx_copy(0).wait_recv()
    v = v + cxr[0].astype(F32)
    for k in range(1, 8):
        c_copy(k).wait_recv()
        v = v + cr[k].astype(F32)
    v_hi = v.astype(BF16)
    v_lo = (v - v_hi.astype(F32)).astype(BF16)
    img_out[rows(own_sub), :] = v_hi

    tr.wait_recv()
    pad = jnp.zeros((kts.shape[0] - ch, kts.shape[1]), BF16)
    dims = (((0,), (0,)), ((), ()))
    keys_s = kts[...]
    part = lax.dot_general(
        keys_s, jnp.concatenate([v_hi, pad], 0), dims, preferred_element_type=F32
    ) + lax.dot_general(
        keys_s, jnp.concatenate([v_lo, pad], 0), dims, preferred_element_type=F32
    )
    spart[...] = part
    n2 = spart.shape[0] // 2
    exs[...] = spart[rows(1 - core, n2), :].astype(BF16)
    ex = send(exs, exr, ex_ss, ex_rs, *partner)
    ex.start()
    ex.wait_recv()
    e1s[...] = (spart[rows(core, n2), :] + exr[...].astype(F32))
    blk = n2 // 8
    e1c = []
    for k in range(1, 8):
        e2s[k] = e1s[rows((g + k) % 8, blk), :].astype(BF16)
        cp = send(e2s.at[k], e1r.at[k], e1_ss.at[k], e1_rs.at[k], *g_to(k))
        cp.start()
        e1c.append(cp)
    dc = {}
    mine = img_out.at[rows(own_sub)]

    def gather(ref_of, ss, rs, out):
        for k in range(1, 8):
            ref = ref_of(g)
            out[k] = send(ref, ref, ss.at[k], rs.at[k], *g_to(k))
            out[k].start()
        ref = ref_of(g)
        out[0] = send(ref, ref, ss.at[0], rs.at[0], *partner)
        out[0].start()

    def relay(ref_of, ss, rs, out):
        for k in range(1, 8):
            out[k].wait_recv()
            ref = ref_of((g - k + 8) % 8)
            out[7 + k] = send(ref, ref, ss.at[7 + k], rs.at[7 + k], *partner)
            out[7 + k].start()

    def img_ref(gg):
        return img_out.at[rows(core * 8 + (gg + 4) % 8)]

    def s_ref(gg):
        return s_out.at[rows(core * 8 + gg, blk)]

    gather(img_ref, d_ss, d_rs, dc)
    v = e1s[rows(g, blk), :]
    for k in range(1, 8):
        e1c[k - 1].wait_recv()
        v = v + e1r[k].astype(F32)
    s2[...] = v
    e1s[pl.ds(0, blk), :] = v
    tile = pl.ds(0, blk)

    def piece(ref, i):
        return ref.at[rows(i // 4, 8), pl.ds(pl.multiple_of(i % 4 * 128, 128), 128)]

    e2c = []
    for k in range(1, 16):
        cp = send(
            piece(e1s, (me_r + k) % 16), e2r.at[k], e2_ss.at[k], e2_rs.at[k],
            (me_r + k) % 16, me_c,
        )
        cp.start()
        e2c.append(cp)
    at_rows = rows(me_r // 4, 8)
    at_cols = pl.ds(pl.multiple_of(me_r % 4 * 128, 128), 128)
    v = e1s[at_rows, at_cols]
    for k in range(1, 16):
        e2c[k - 1].wait_recv()
        v = v + e2r[k]
    e3[...] = v
    e3c = []
    for k in range(1, 16):
        cp = send(
            e3, s2.at[at_rows, at_cols], e3_ss.at[k], e3_rs.at[k],
            (me_r + k) % 16, me_c,
        )
        cp.start()
        e3c.append(cp)
    s2[at_rows, at_cols] = v
    for cp in e3c:
        cp.wait_recv()
    s_out[rows(core * 8 + g, blk), :] = s2[...]
    ec = {}
    gather(s_ref, e4_ss, e4_rs, ec)
    relay(s_ref, e4_ss, e4_rs, ec)
    relay(img_ref, d_ss, d_rs, dc)
    for out in (ec, dc):
        out[0].wait_recv()
        for k in range(1, 8):
            out[7 + k].wait_recv()
    pending += [ex] + e1c + e2c + e3c + list(ec.values()) + list(dc.values())
    for cp in pending:
        cp.wait_send()
    for k in range(8):
        cx_copy(k).wait_send()
    for k in range(1, 8):
        c_copy(k).wait_send()


def exchange(gate, up, inv_cov):
    ff, facts = gate.shape
    ch, half, blk = ff // 16, facts // 2, facts // 16
    dma = pltpu.SemaphoreType.DMA
    vm = pltpu.VMEM
    scratch = [
        vm(inv_cov.shape, BF16),
        vm((8, 2, ch, half), BF16), vm((8, 2, ch, half), BF16),
        vm((7, 2, ch, half), BF16), vm((7, 2, ch, half), BF16),
        vm((7, 2, 2, ch, half), BF16), vm((7, 2, 2, ch, half), BF16),
        vm((2, ch, half), F32), vm((2, ch, half), F32),
        vm((ff, facts), BF16), vm((-(-ch // 128) * 128, facts), BF16),
        vm((8, ch, facts), BF16), vm((8, ch, facts), BF16),
        vm((8, ch, facts), BF16), vm((8, ch, facts), BF16),
        vm((facts, facts), F32),
        vm((facts // 2, facts), BF16), vm((facts // 2, facts), BF16),
        vm((facts // 2, facts), F32), vm((8, blk, facts), BF16),
        vm((8, blk, facts), BF16), vm((16, 8, 128), F32), vm((8, 128), F32),
        vm((blk, facts), F32),
        dma(()), dma((8,)), dma((8,)), dma((24,)), dma((24,)), dma(()), dma(()),
        dma((41,)), dma((41,)), dma(()), dma(()),
        dma((8,)), dma((8,)), dma((8,)), dma((8,)), dma(()), dma(()),
        dma((8,)), dma((8,)), dma((16,)), dma((16,)), dma((16,)), dma((16,)),
        dma((15,)), dma((15,)), dma((15,)), dma((15,)), dma(()),
    ]
    return pl.pallas_call(
        exchange_kernel,
        name="exchange",
        out_shape=(
            jax.ShapeDtypeStruct((facts, facts), F32),
            jax.ShapeDtypeStruct((ff, facts), BF16),
        ),
        in_specs=[
            pl.BlockSpec(memory_space=pltpu.VMEM),
            pl.BlockSpec(memory_space=pltpu.VMEM),
            pl.BlockSpec(memory_space=pl.ANY),
        ],
        out_specs=[pl.BlockSpec(memory_space=pltpu.VMEM)] * 2,
        scratch_shapes=scratch,
        compiler_params=pltpu.CompilerParams(
            collective_id=0, has_side_effects=True, vmem_limit_bytes=60 * 2**20
        ),
    )(gate, up, inv_cov)


def invert(m):
    n = m.shape[0]
    lane = lax.broadcasted_iota(jnp.int32, (1, n), 1)
    sub = lax.broadcasted_iota(jnp.int32, (n, 1), 0)
    for p in range(0, n, 2):
        q = p + 1
        row_p, row_q = m[p:q, :], m[q : q + 1, :]
        col_p, col_q = m[:, p:q], m[:, q : q + 1]
        a = jnp.broadcast_to(m[p:q, p:q], (1, n))
        b = jnp.broadcast_to(m[p:q, q : q + 1], (1, n))
        d = jnp.broadcast_to(m[q : q + 1, q : q + 1], (1, n))
        r = 1.0 / (a * d - b * b)
        a, b, d = d * r, -b * r, a * r
        new_p = jnp.where(lane == p, a, jnp.where(lane == q, b, a * row_p + b * row_q))
        new_q = jnp.where(lane == p, b, jnp.where(lane == q, d, b * row_p + d * row_q))
        rest = jnp.where((lane == p) | (lane == q), 0.0, m)
        m = jnp.where(
            sub == p, new_p,
            jnp.where(sub == q, new_q, rest - col_p * new_p - col_q * new_q),
        )
    return m


def solve_kernel(s_ref, t_ref, img_ref, out_ref, a):
    n = s_ref.shape[0]
    b = min(128, n)
    eye = lax.broadcasted_iota(jnp.int32, (n, n), 0) == lax.broadcasted_iota(
        jnp.int32, (n, n), 1
    )
    a[...] = s_ref[...] + jnp.where(eye, 1.0, 0.0)

    def dot(p, q):
        return jnp.dot(p, q, precision=lax.Precision.HIGHEST, preferred_element_type=F32)

    def block(k, carry):
        d = pl.ds(pl.multiple_of(k * b, b), b)
        inv = invert(a[d, d])
        col = a[:, d]
        wide = dot(inv, a[d, :])
        a[...] = a[...] - dot(col, wide)
        a[:, d] = -dot(col, inv)
        a[d, :] = wide
        a[d, d] = inv
        return carry

    lax.fori_loop(0, n // b, block, 0)
    v = a[...]
    coeffs = jnp.zeros((t_ref.shape[0], n), F32)
    for _ in range(3):
        short = v.astype(BF16)
        coeffs = coeffs + jnp.dot(t_ref[...], short, preferred_element_type=F32)
        v = v - short.astype(F32)
    coeffs = coeffs.astype(BF16)
    w = 256
    for j in range(out_ref.shape[1] // w):
        out_ref[:, j * w : (j + 1) * w] = lax.dot_general(
            coeffs, img_ref[j * w : (j + 1) * w, :], (((1,), (1,)), ((), ())),
            preferred_element_type=F32,
        ).astype(BF16)


def solve(system, target, image_t):
    n = system.shape[0]
    return pl.pallas_call(
        solve_kernel,
        name="solve",
        out_shape=jax.ShapeDtypeStruct((target.shape[0], image_t.shape[0]), BF16),
        in_specs=[pl.BlockSpec(memory_space=pltpu.VMEM)] * 3,
        out_specs=pl.BlockSpec(memory_space=pltpu.VMEM),
        scratch_shapes=[pltpu.VMEM((n, n), F32)],
        compiler_params=pltpu.CompilerParams(vmem_limit_bytes=40 * 2**20),
    )(system, target, image_t)


def per_device(hidden, positions, gate_weight, up_weight, inv_cov, target_res):
    tokens = lax.broadcasted_iota(jnp.int32, (positions.shape[0], hidden.shape[0]), 1)
    chosen = (positions[:, None] == tokens).astype(BF16)
    subject = lax.dot_general(
        hidden, chosen, (((0,), (1,)), ((), ())), preferred_element_type=F32
    ).astype(BF16)
    dims = (((0,), (0,)), ((), ()))
    gate = lax.dot_general(gate_weight, subject, dims, preferred_element_type=F32)
    up = lax.dot_general(up_weight, subject, dims, preferred_element_type=F32)
    system, image_t = exchange(gate, up, inv_cov)
    return solve(system, target_res, image_t)


def solution(mesh):
    return jax.shard_map(
        per_device,
        mesh=mesh,
        in_specs=(
            P(None, "row"),
            P(),
            P("row", "col"),
            P("row", "col"),
            P("row", "col"),
            P("col", None),
        ),
        out_specs=P("col", "row"),
        check_vma=False,
    )
```

```python
import jax
import jax.numpy as jnp
from jax import lax
from jax.experimental import pallas as pl
from jax.experimental.pallas import tpu as pltpu
from jax.sharding import PartitionSpec as P

MESH = pl.DeviceIdType.MESH
F32 = jnp.float32
BF16 = jnp.bfloat16


def invert(m):
    n = m.shape[0]
    lane = lax.broadcasted_iota(jnp.int32, (1, n), 1)
    sub = lax.broadcasted_iota(jnp.int32, (n, 1), 0)
    for p in range(0, n, 4):
        row = [m[p + i : p + i + 1, :] for i in range(4)]
        col = [m[:, p + i : p + i + 1] for i in range(4)]

        def at(i, j):
            return jnp.broadcast_to(row[i][:, p + j : p + j + 1], (1, n))

        a, b, d = at(0, 0), at(0, 1), at(1, 1)
        r = 1.0 / (a * d - b * b)
        a, b, d = d * r, -b * r, a * r
        c = [[at(0, 2), at(0, 3)], [at(1, 2), at(1, 3)]]
        e = [[a * c[0][j] + b * c[1][j] for j in (0, 1)],
             [b * c[0][j] + d * c[1][j] for j in (0, 1)]]
        s0 = at(2, 2) - (c[0][0] * e[0][0] + c[1][0] * e[1][0])
        s1 = at(2, 3) - (c[0][0] * e[0][1] + c[1][0] * e[1][1])
        s2 = at(3, 3) - (c[0][1] * e[0][1] + c[1][1] * e[1][1])
        r = 1.0 / (s0 * s2 - s1 * s1)
        s0, s1, s2 = s2 * r, -s1 * r, s0 * r
        f = [[e[i][0] * s0 + e[i][1] * s1, e[i][0] * s1 + e[i][1] * s2] for i in (0, 1)]
        top = [[None, None], [None, None]]
        for i in (0, 1):
            for j in (0, 1):
                base = ((a, b), (b, d))[i][j]
                top[i][j] = base + f[i][0] * e[j][0] + f[i][1] * e[j][1]
        inv = [
            [top[0][0], top[0][1], -f[0][0], -f[0][1]],
            [top[1][0], top[1][1], -f[1][0], -f[1][1]],
            [-f[0][0], -f[1][0], s0, s1],
            [-f[0][1], -f[1][1], s1, s2],
        ]
        new = []
        for i in range(4):
            v = (inv[i][0] * row[0] + inv[i][1] * row[1]) + (
                inv[i][2] * row[2] + inv[i][3] * row[3]
            )
            for j in range(4):
                v = jnp.where(lane == p + j, inv[i][j], v)
            new.append(v)
        rest = jnp.where((lane >= p) & (lane < p + 4), 0.0, m)
        m = rest - (col[0] * new[0] + col[1] * new[1]) - (
            col[2] * new[2] + col[3] * new[3]
        )
        for i in range(4):
            m = jnp.where(sub == p + i, new[i], m)
    return m


def right_solve(system, a, target, between):
    n = a.shape[0]
    b = n // 4
    eye = lax.broadcasted_iota(jnp.int32, (n, n), 0) == lax.broadcasted_iota(
        jnp.int32, (n, n), 1
    )
    a[...] = system[...] + jnp.where(eye, 1.0, 0.0)

    def dot(p, q):
        return jnp.dot(p, q, precision=lax.Precision.HIGHEST, preferred_element_type=F32)

    def block(k, carry):
        pl.when(k == 2)(between)
        d = pl.ds(pl.multiple_of(k * b, b), b)
        inv = invert(a[d, d])
        col = a[:, d]
        wide = dot(inv, a[d, :])
        a[...] = a[...] - dot(col, wide)
        a[:, d] = -dot(col, inv)
        a[d, :] = wide
        a[d, d] = inv
        return carry

    lax.fori_loop(0, 4, block, 0)
    v = a[...]
    coeffs = jnp.zeros((target.shape[0], n), F32)
    for _ in range(3):
        short = v.astype(BF16)
        coeffs = coeffs + jnp.dot(target[...], short, preferred_element_type=F32)
        v = v - short.astype(F32)
    return coeffs.astype(BF16)


def exchange_kernel(
    subject, target, gate_hbm, up_hbm, cov_hbm, coeffs_out, img_out, s_out, work,
    weights, proj, cov, ysend, yrecv, psend, precv, qsend, qrecv, qy_s, qy_r,
    kt, kts, cxs, cxr, cs, cr, spart, exs, exr, e1s, e1r, e2s, e2r, e3, s2,
    w_sem, cov_sem, y_ss, y_rs, z_ss, z_rs, qy_ss, qy_rs, b_ss, b_rs, t_ss, t_rs,
    cx_ss, cx_rs, c_ss, c_rs, ex_ss, ex_rs, e1_ss, e1_rs, e2_ss, e2_rs,
    e3_ss, e3_rs, e4_ss, e4_rs, d_ss, d_rs, loc_sem,
):
    ch = kt.shape[0] // 16
    half = kt.shape[1] // 2
    me_r, me_c = lax.axis_index("row"), lax.axis_index("col")
    y, z = me_r // 8, me_r % 8
    g, core = me_c // 2, me_c % 2

    def send(src, dst, ss, rs, r, c):
        return pltpu.make_async_remote_copy(
            src_ref=src, dst_ref=dst, send_sem=ss, recv_sem=rs,
            device_id=(r, c), device_id_type=MESH,
        )

    def rows(i, n=ch):
        return pl.ds(pl.multiple_of(i * n, 8), n)

    y_to = ((1 - y) * 8 + z, me_c)

    def z_to(step):
        return (y * 8 + (z + step + 8) % 8, me_c)

    partner = (me_r, g * 2 + 1 - core)

    def g_to(k):
        return (me_r, ((g + k) % 8) * 2 + core)

    own_sub = core * 8 + (g + 4) % 8
    t_out = (me_c, ((me_r % 8 + 4) % 8) * 2 + me_r // 8)
    t_in = (own_sub, me_r)

    loads = [
        pltpu.make_async_copy(gate_hbm, weights.at[0], w_sem.at[0]),
        pltpu.make_async_copy(up_hbm, weights.at[1], w_sem.at[1]),
    ]
    cov_copy = pltpu.make_async_copy(cov_hbm, cov, cov_sem)
    for cp in loads + [cov_copy]:
        cp.start()

    kts[...] = jnp.zeros_like(kts)
    barrier = pltpu.get_barrier_semaphore()
    peers = [((me_r + k) % 16, me_c) for k in range(1, 16)]
    peers += [g_to(k) for k in range(1, 8)] + [partner, t_out, t_in]
    for p in peers:
        pl.semaphore_signal(barrier, inc=1, device_id=p, device_id_type=MESH)
    lo, hi = pl.ds(0, half), pl.ds(half, half)
    pending = []
    width = proj.shape[1] // 7

    def project(i):
        def step(j, carry):
            at = pl.ds(pl.multiple_of(j * width, width), width)
            proj[i, at, :] = lax.dot_general(
                weights[i, :, at], subject[...], (((0,), (0,)), ((), ())),
                preferred_element_type=F32,
            )
            return carry

        loads[i].wait()
        lax.fori_loop(0, 7, step, 0)

    project(0)
    project(1)

    def projections(r, lanes):
        return proj[:, rows(r), lanes]

    order = (4, 3, 5, 2, 6, 1, 7, 0)
    for o in order:
        ysend[o] = projections((1 - y) * 8 + (z + o) % 8, lo).astype(BF16)
    pl.semaphore_wait(barrier, len(peers))
    ycopies = {}
    for o in order:
        ycopies[o] = send(ysend.at[o], yrecv.at[o], y_ss.at[o], y_rs.at[o], *y_to)
        ycopies[o].start()

    def p_own(o):
        return projections(y * 8 + (z + o) % 8, lo) + yrecv[o].astype(F32)

    def q_own(o, yy):
        return projections(yy * 8 + (z + o) % 8, hi)

    copies = {}
    for s in range(1, 5):
        for chain in range(3):
            for side in (0, 1):
                if side == 1 and s == 1:
                    continue
                slot = side * 4 + s - 1 - side
                sign = (-1 if side == 0 else 1) * (-1 if chain == 2 else 1)
                o = (sign * (5 - s)) % 8
                if chain == 2:
                    ycopies[o].wait_recv()
                    v = p_own(o)
                    src, dst = psend.at[slot], precv
                else:
                    v = q_own(o, chain)
                    src, dst = qsend.at[slot, chain], qrecv.at[:, chain]
                if s > 1 + side:
                    copies[chain, side, s - 1].wait_recv()
                    v = v + dst[slot - 1].astype(F32)
                src[...] = v.astype(BF16)
                i = chain * 8 + side * 4 + s - 1
                cp = send(src, dst.at[slot], z_ss.at[i], z_rs.at[i], *z_to(sign))
                cp.start()
                copies[chain, side, s] = cp
    for chain in (0, 1):
        copies[chain, 0, 4].wait_recv()
        copies[chain, 1, 4].wait_recv()

    def q_sum(yy):
        return q_own(0, yy) + qrecv[3, yy].astype(F32) + qrecv[6, yy].astype(F32)

    qy_s[...] = q_sum(1 - y)
    qy = send(qy_s, qy_r, qy_ss, qy_rs, *y_to)
    qy.start()
    ycopies[0].wait_recv()
    copies[2, 0, 4].wait_recv()
    copies[2, 1, 4].wait_recv()
    v = p_own(0) + precv[3].astype(F32) + precv[6].astype(F32)
    kt[rows(me_r), lo] = (v[0] / (1.0 + jnp.exp(-v[0])) * v[1]).astype(BF16)
    v = q_sum(y)
    qy.wait_recv()
    v = v + qy_r[...]
    kt[rows(me_r), hi] = (v[0] / (1.0 + jnp.exp(-v[0])) * v[1]).astype(BF16)
    pending += list(ycopies.values()) + list(copies.values()) + [qy]

    def shard(zo, rel):
        yy = y if rel == 0 else 1 - y
        return rows(yy * 8 + (zo + 8) % 8)

    mine = kt.at[rows(me_r)]
    bc = {}

    def share(ref, i, to, key):
        bc[key] = send(ref, ref, b_ss.at[i], b_rs.at[i], *to)
        bc[key].start()

    def forward(h, side, t, rel):
        sign = 1 if h == side else -1
        ref = kt.at[shard(z - sign * (t - 1), rel), lo if h == 0 else hi]
        share(ref, h * 16 + side * 8 + (t - 1) * 2 + rel, z_to(sign), (h, side, t, rel))

    def across(side, t):
        zo = z + (t if side == 0 else -t)
        share(kt.at[shard(zo, 0), hi], 33 + side * 4 + t, y_to, ("y", side, t))

    share(kt.at[rows(me_r), lo], 32, y_to, "y")
    for side in (0, 1):
        forward(0, side, 1, 0)
        forward(1, side, 1, 0)
    across(0, 0)
    bc["y"].wait_recv()
    for side in (0, 1):
        forward(0, side, 1, 1)
    for t in range(2, 6):
        for h, rel in ((0, 0), (1, 0), (0, 1)):
            for side in (0, 1):
                if t - 1 > 4 - side:
                    continue
                bc[h, side, t - 1, rel].wait_recv()
                if t <= 4 - side:
                    forward(h, side, t, rel)
                if h == 1:
                    across(side, t - 1)
    for key in list(bc):
        if key != "y" and key[0] == "y":
            bc[key].wait_recv()
    tr = send(mine, kts.at[pl.ds(0, ch)], t_ss, t_rs, *t_out)
    tr.start()
    pending += [tr] + list(bc.values())

    cov_copy.wait()

    def product(sub):
        return jnp.dot(cov[rows(sub), :], kt[...], preferred_element_type=F32)

    def sub_of(k, cc):
        return cc * 8 + (g + k + 4) % 8

    def cx_copy(k):
        return send(cxs.at[k], cxr.at[k], cx_ss.at[k], cx_rs.at[k], *partner)

    def c_copy(k):
        return send(cs.at[k], cr.at[k], c_ss.at[k], c_rs.at[k], *g_to(k))

    def far(k):
        cxs[k] = product(sub_of(k, 1 - core)).astype(BF16)
        cx_copy(k).start()

    def near(k):
        v = product(sub_of(k, core))
        cx_copy(k).wait_recv()
        cs[k] = (v + cxr[k].astype(F32)).astype(BF16)
        c_copy(k).start()

    def step(k, carry):
        far((k + 3) % 8)
        near(k + 1)
        return carry

    far(1)
    far(2)
    lax.fori_loop(0, 6, step, 0)
    near(7)
    v = product(sub_of(0, core))
    cx_copy(0).wait_recv()
    v = v + cxr[0].astype(F32)
    for k in range(1, 8):
        c_copy(k).wait_recv()
        v = v + cr[k].astype(F32)
    v_hi = v.astype(BF16)
    v_lo = (v - v_hi.astype(F32)).astype(BF16)
    img_out[rows(own_sub), :] = v_hi

    tr.wait_recv()
    pad = jnp.zeros((kts.shape[0] - ch, kts.shape[1]), BF16)
    dims = (((0,), (0,)), ((), ()))
    keys_s = kts[...]
    part = lax.dot_general(
        keys_s, jnp.concatenate([v_hi, pad], 0), dims, preferred_element_type=F32
    ) + lax.dot_general(
        keys_s, jnp.concatenate([v_lo, pad], 0), dims, preferred_element_type=F32
    )
    spart[...] = part
    n2 = spart.shape[0] // 2
    exs[...] = spart[rows(1 - core, n2), :].astype(BF16)
    ex = send(exs, exr, ex_ss, ex_rs, *partner)
    ex.start()
    ex.wait_recv()
    e1s[...] = (spart[rows(core, n2), :] + exr[...].astype(F32))
    blk = n2 // 8
    e1c = []
    for k in range(1, 8):
        e2s[k] = e1s[rows((g + k) % 8, blk), :].astype(BF16)
        cp = send(e2s.at[k], e1r.at[k], e1_ss.at[k], e1_rs.at[k], *g_to(k))
        cp.start()
        e1c.append(cp)
    dc = {}
    mine = img_out.at[rows(own_sub)]

    def gather(ref_of, ss, rs, out):
        for k in range(1, 8):
            ref = ref_of(g)
            out[k] = send(ref, ref, ss.at[k], rs.at[k], *g_to(k))
            out[k].start()
        ref = ref_of(g)
        out[0] = send(ref, ref, ss.at[0], rs.at[0], *partner)
        out[0].start()

    def relay(ref_of, ss, rs, out):
        for k in range(1, 8):
            out[k].wait_recv()
            ref = ref_of((g - k + 8) % 8)
            out[7 + k] = send(ref, ref, ss.at[7 + k], rs.at[7 + k], *partner)
            out[7 + k].start()

    def img_ref(gg):
        return img_out.at[rows(core * 8 + (gg + 4) % 8)]

    def s_ref(gg):
        return s_out.at[rows(core * 8 + gg, blk)]

    v = e1s[rows(g, blk), :]
    for k in range(1, 8):
        e1c[k - 1].wait_recv()
        v = v + e1r[k].astype(F32)
    s2[...] = v
    e1s[pl.ds(0, blk), :] = v
    tile = pl.ds(0, blk)

    def piece(ref, i):
        return ref.at[rows(i // 4, 8), pl.ds(pl.multiple_of(i % 4 * 128, 128), 128)]

    e2c = []
    for k in range(1, 16):
        cp = send(
            piece(e1s, (me_r + k) % 16), e2r.at[k], e2_ss.at[k], e2_rs.at[k],
            (me_r + k) % 16, me_c,
        )
        cp.start()
        e2c.append(cp)
    at_rows = rows(me_r // 4, 8)
    at_cols = pl.ds(pl.multiple_of(me_r % 4 * 128, 128), 128)
    v = e1s[at_rows, at_cols]
    for k in range(1, 16):
        e2c[k - 1].wait_recv()
        v = v + e2r[k]
    e3[...] = v
    e3c = []
    for k in range(1, 16):
        cp = send(
            e3, s2.at[at_rows, at_cols], e3_ss.at[k], e3_rs.at[k],
            (me_r + k) % 16, me_c,
        )
        cp.start()
        e3c.append(cp)
    s2[at_rows, at_cols] = v
    for cp in e3c:
        cp.wait_recv()
    s_out[rows(core * 8 + g, blk), :] = s2[...]
    ec = {}
    gather(s_ref, e4_ss, e4_rs, ec)
    relay(s_ref, e4_ss, e4_rs, ec)
    gather(img_ref, d_ss, d_rs, dc)
    ec[0].wait_recv()
    for k in range(1, 8):
        ec[7 + k].wait_recv()

    def d_relay(k):
        ref = img_ref((g - k + 8) % 8)
        return send(ref, ref, d_ss.at[7 + k], d_rs.at[7 + k], *partner)

    def relay_images():
        for k in range(1, 8):
            dc[k].wait_recv()
            d_relay(k).start()

    coeffs_out[...] = right_solve(s_out, work, target, relay_images)
    dc[0].wait_recv()
    for k in range(1, 8):
        d_relay(k).wait()
    pending += [ex] + e1c + e2c + e3c + list(ec.values()) + list(dc.values())
    for cp in pending:
        cp.wait_send()
    for k in range(8):
        cx_copy(k).wait_send()
    for k in range(1, 8):
        c_copy(k).wait_send()


def exchange(subject, target, gate_weight, up_weight, inv_cov):
    ff, facts = gate_weight.shape[1], subject.shape[1]
    ch, half, blk = ff // 16, facts // 2, facts // 16
    dma = pltpu.SemaphoreType.DMA
    vm = pltpu.VMEM
    scratch = [
        vm((facts, facts), F32), vm((facts, facts), F32), vm((2,) + gate_weight.shape, BF16),
        vm((2, ff, facts), F32), vm(inv_cov.shape, BF16),
        vm((8, 2, ch, half), BF16), vm((8, 2, ch, half), BF16),
        vm((7, 2, ch, half), BF16), vm((7, 2, ch, half), BF16),
        vm((7, 2, 2, ch, half), BF16), vm((7, 2, 2, ch, half), BF16),
        vm((2, ch, half), F32), vm((2, ch, half), F32),
        vm((ff, facts), BF16), vm((-(-ch // 128) * 128, facts), BF16),
        vm((8, ch, facts), BF16), vm((8, ch, facts), BF16),
        vm((8, ch, facts), BF16), vm((8, ch, facts), BF16),
        vm((facts, facts), F32),
        vm((facts // 2, facts), BF16), vm((facts // 2, facts), BF16),
        vm((facts // 2, facts), F32), vm((8, blk, facts), BF16),
        vm((8, blk, facts), BF16), vm((16, 8, 128), F32), vm((8, 128), F32),
        vm((blk, facts), F32),
        dma((2,)), dma(()), dma((8,)), dma((8,)), dma((24,)), dma((24,)), dma(()), dma(()),
        dma((41,)), dma((41,)), dma(()), dma(()),
        dma((8,)), dma((8,)), dma((8,)), dma((8,)), dma(()), dma(()),
        dma((8,)), dma((8,)), dma((16,)), dma((16,)), dma((16,)), dma((16,)),
        dma((15,)), dma((15,)), dma((15,)), dma((15,)), dma(()),
    ]
    return pl.pallas_call(
        exchange_kernel,
        name="exchange",
        out_shape=(
            jax.ShapeDtypeStruct(target.shape, BF16),
            jax.ShapeDtypeStruct((ff, facts), BF16),
        ),
        in_specs=[
            pl.BlockSpec(memory_space=pltpu.VMEM),
            pl.BlockSpec(memory_space=pltpu.VMEM),
            pl.BlockSpec(memory_space=pl.ANY),
            pl.BlockSpec(memory_space=pl.ANY),
            pl.BlockSpec(memory_space=pl.ANY),
        ],
        out_specs=[pl.BlockSpec(memory_space=pltpu.VMEM)] * 2,
        scratch_shapes=scratch,
        compiler_params=pltpu.CompilerParams(
            collective_id=0, has_side_effects=True, vmem_limit_bytes=60 * 2**20
        ),
    )(subject, target, gate_weight, up_weight, inv_cov)


def per_device(hidden, positions, gate_weight, up_weight, inv_cov, target_res):
    tokens = lax.broadcasted_iota(jnp.int32, (positions.shape[0], hidden.shape[0]), 1)
    chosen = (positions[:, None] == tokens).astype(BF16)
    subject = lax.dot_general(
        hidden, chosen, (((0,), (1,)), ((), ())), preferred_element_type=F32
    ).astype(BF16)
    coeffs, image_t = exchange(subject, target_res, gate_weight, up_weight, inv_cov)
    return lax.dot_general(
        coeffs, image_t, (((1,), (1,)), ((), ())), preferred_element_type=F32
    ).astype(BF16)


def solution(mesh):
    return jax.shard_map(
        per_device,
        mesh=mesh,
        in_specs=(
            P(None, "row"),
            P(),
            P("row", "col"),
            P("row", "col"),
            P("row", "col"),
            P("col", None),
        ),
        out_specs=P("col", "row"),
        check_vma=False,
    )
```

```python
import jax
import jax.numpy as jnp
from jax import lax
from jax.experimental import pallas as pl
from jax.experimental.pallas import tpu as pltpu
from jax.sharding import PartitionSpec as P

MESH = pl.DeviceIdType.MESH
F32 = jnp.float32
BF16 = jnp.bfloat16


def invert(m):
    n = m.shape[0]
    lane = lax.broadcasted_iota(jnp.int32, (1, n), 1)
    sub = lax.broadcasted_iota(jnp.int32, (n, 1), 0)
    for p in range(0, n, 4):
        row = [m[p + i : p + i + 1, :] for i in range(4)]
        col = [m[:, p + i : p + i + 1] for i in range(4)]

        def at(i, j):
            return jnp.broadcast_to(row[i][:, p + j : p + j + 1], (1, n))

        a, b, d = at(0, 0), at(0, 1), at(1, 1)
        r = 1.0 / (a * d - b * b)
        a, b, d = d * r, -b * r, a * r
        c = [[at(0, 2), at(0, 3)], [at(1, 2), at(1, 3)]]
        e = [[a * c[0][j] + b * c[1][j] for j in (0, 1)],
             [b * c[0][j] + d * c[1][j] for j in (0, 1)]]
        s0 = at(2, 2) - (c[0][0] * e[0][0] + c[1][0] * e[1][0])
        s1 = at(2, 3) - (c[0][0] * e[0][1] + c[1][0] * e[1][1])
        s2 = at(3, 3) - (c[0][1] * e[0][1] + c[1][1] * e[1][1])
        r = 1.0 / (s0 * s2 - s1 * s1)
        s0, s1, s2 = s2 * r, -s1 * r, s0 * r
        f = [[e[i][0] * s0 + e[i][1] * s1, e[i][0] * s1 + e[i][1] * s2] for i in (0, 1)]
        top = [[None, None], [None, None]]
        for i in (0, 1):
            for j in (0, 1):
                base = ((a, b), (b, d))[i][j]
                top[i][j] = base + f[i][0] * e[j][0] + f[i][1] * e[j][1]
        inv = [
            [top[0][0], top[0][1], -f[0][0], -f[0][1]],
            [top[1][0], top[1][1], -f[1][0], -f[1][1]],
            [-f[0][0], -f[1][0], s0, s1],
            [-f[0][1], -f[1][1], s1, s2],
        ]
        new = []
        for i in range(4):
            v = (inv[i][0] * row[0] + inv[i][1] * row[1]) + (
                inv[i][2] * row[2] + inv[i][3] * row[3]
            )
            for j in range(4):
                v = jnp.where(lane == p + j, inv[i][j], v)
            new.append(v)
        rest = jnp.where((lane >= p) & (lane < p + 4), 0.0, m)
        m = rest - (col[0] * new[0] + col[1] * new[1]) - (
            col[2] * new[2] + col[3] * new[3]
        )
        for i in range(4):
            m = jnp.where(sub == p + i, new[i], m)
    return m


def right_solve(system, a, pivot, target, between):
    n = a.shape[0]
    b = n // 4
    eye = lax.broadcasted_iota(jnp.int32, (n, n), 0) == lax.broadcasted_iota(
        jnp.int32, (n, n), 1
    )
    a[...] = system[...] + jnp.where(eye, 1.0, 0.0)

    def dot(p, q):
        return jnp.dot(p, q, precision=lax.Precision.HIGHEST, preferred_element_type=F32)

    def block(k, carry):
        pl.when(k == 2)(between)
        d = pl.ds(pl.multiple_of(k * b, b), b)
        @pl.when(k < 4)
        def _():
            pivot[...] = invert(a[d, d])

        inv = pivot[...]
        col = a[:, d]
        wide = dot(inv, a[d, :])
        a[...] = a[...] - dot(col, wide)
        a[:, d] = -dot(col, inv)
        a[d, :] = wide
        a[d, d] = inv
        return carry

    lax.fori_loop(0, 4, block, 0)
    v = a[...]
    coeffs = jnp.zeros((target.shape[0], n), F32)
    for _ in range(3):
        short = v.astype(BF16)
        coeffs = coeffs + jnp.dot(target[...], short, preferred_element_type=F32)
        v = v - short.astype(F32)
    return coeffs.astype(BF16)


def exchange_kernel(
    subject, target, gate_hbm, up_hbm, cov_hbm, coeffs_out, img_out, s_out, work, pivot,
    weights, proj, cov, ysend, yrecv, psend, precv, qsend, qrecv, qy_s, qy_r,
    kt, kts, cxs, cxr, cs, cr, exs, exr, e1s, e1r, e2s, e2r, e3, s2,
    w_sem, cov_sem, y_ss, y_rs, z_ss, z_rs, qy_ss, qy_rs, b_ss, b_rs, t_ss, t_rs,
    cx_ss, cx_rs, c_ss, c_rs, ex_ss, ex_rs, e1_ss, e1_rs, e2_ss, e2_rs,
    e3_ss, e3_rs, e4_ss, e4_rs, d_ss, d_rs, loc_sem,
):
    ch = kt.shape[0] // 16
    half = kt.shape[1] // 2
    me_r, me_c = lax.axis_index("row"), lax.axis_index("col")
    y, z = me_r // 8, me_r % 8
    g, core = me_c // 2, me_c % 2

    def send(src, dst, ss, rs, r, c):
        return pltpu.make_async_remote_copy(
            src_ref=src, dst_ref=dst, send_sem=ss, recv_sem=rs,
            device_id=(r, c), device_id_type=MESH,
        )

    def rows(i, n=ch):
        return pl.ds(pl.multiple_of(i * n, 8), n)

    y_to = ((1 - y) * 8 + z, me_c)

    def z_to(step):
        return (y * 8 + (z + step + 8) % 8, me_c)

    partner = (me_r, g * 2 + 1 - core)

    def g_to(k):
        return (me_r, ((g + k) % 8) * 2 + core)

    own_sub = core * 8 + (g + 4) % 8
    t_out = (me_c, ((me_r % 8 + 4) % 8) * 2 + me_r // 8)
    t_in = (own_sub, me_r)

    loads = [
        pltpu.make_async_copy(gate_hbm, weights.at[0], w_sem.at[0]),
        pltpu.make_async_copy(up_hbm, weights.at[1], w_sem.at[1]),
    ]
    cov_copy = pltpu.make_async_copy(cov_hbm, cov, cov_sem)
    for cp in loads:
        cp.start()

    kts[...] = jnp.zeros_like(kts)
    barrier = pltpu.get_barrier_semaphore()
    peers = [((me_r + k) % 16, me_c) for k in range(1, 16)]
    peers += [g_to(k) for k in range(1, 8)] + [partner, t_out, t_in]
    for p in peers:
        pl.semaphore_signal(barrier, inc=1, device_id=p, device_id_type=MESH)
    lo, hi = pl.ds(0, half), pl.ds(half, half)
    pending = []
    width = proj.shape[1] // 7

    def project(i):
        def step(j, carry):
            at = pl.ds(pl.multiple_of(j * width, width), width)
            proj[i, at, :] = lax.dot_general(
                weights[i, :, at], subject[...], (((0,), (0,)), ((), ())),
                preferred_element_type=F32,
            )
            return carry

        loads[i].wait()
        lax.fori_loop(0, 7, step, 0)

    project(0)
    cov_copy.start()
    project(1)

    def projections(r, lanes):
        return proj[:, rows(r), lanes]

    order = (4, 3, 5, 2, 6, 1, 7, 0)
    for o in order:
        ysend[o] = projections((1 - y) * 8 + (z + o) % 8, lo).astype(BF16)
    pl.semaphore_wait(barrier, len(peers))
    ycopies = {}
    for o in order:
        ycopies[o] = send(ysend.at[o], yrecv.at[o], y_ss.at[o], y_rs.at[o], *y_to)
        ycopies[o].start()

    def p_own(o):
        return projections(y * 8 + (z + o) % 8, lo) + yrecv[o].astype(F32)

    def q_own(o, yy):
        return projections(yy * 8 + (z + o) % 8, hi)

    copies = {}
    for s in range(1, 5):
        for chain in range(3):
            for side in (0, 1):
                if side == 1 and s == 1:
                    continue
                slot = side * 4 + s - 1 - side
                sign = (-1 if side == 0 else 1) * (-1 if chain == 2 else 1)
                o = (sign * (5 - s)) % 8
                if chain == 2:
                    ycopies[o].wait_recv()
                    v = p_own(o)
                    src, dst = psend.at[slot], precv
                else:
                    v = q_own(o, chain)
                    src, dst = qsend.at[slot, chain], qrecv.at[:, chain]
                if s > 1 + side:
                    copies[chain, side, s - 1].wait_recv()
                    v = v + dst[slot - 1].astype(F32)
                src[...] = v.astype(BF16)
                i = chain * 8 + side * 4 + s - 1
                cp = send(src, dst.at[slot], z_ss.at[i], z_rs.at[i], *z_to(sign))
                cp.start()
                copies[chain, side, s] = cp
    for chain in (0, 1):
        copies[chain, 0, 4].wait_recv()
        copies[chain, 1, 4].wait_recv()

    def q_sum(yy):
        return q_own(0, yy) + qrecv[3, yy].astype(F32) + qrecv[6, yy].astype(F32)

    qy_s[...] = q_sum(1 - y)
    qy = send(qy_s, qy_r, qy_ss, qy_rs, *y_to)
    qy.start()
    ycopies[0].wait_recv()
    copies[2, 0, 4].wait_recv()
    copies[2, 1, 4].wait_recv()
    v = p_own(0) + precv[3].astype(F32) + precv[6].astype(F32)
    kt[rows(me_r), lo] = (v[0] / (1.0 + jnp.exp(-v[0])) * v[1]).astype(BF16)
    v = q_sum(y)
    qy.wait_recv()
    v = v + qy_r[...]
    kt[rows(me_r), hi] = (v[0] / (1.0 + jnp.exp(-v[0])) * v[1]).astype(BF16)
    pending += list(ycopies.values()) + list(copies.values()) + [qy]

    def shard(zo, rel):
        yy = y if rel == 0 else 1 - y
        return rows(yy * 8 + (zo + 8) % 8)

    mine = kt.at[rows(me_r)]
    bc = {}

    def share(ref, i, to, key):
        bc[key] = send(ref, ref, b_ss.at[i], b_rs.at[i], *to)
        bc[key].start()

    def forward(h, side, t, rel):
        sign = 1 if h == side else -1
        ref = kt.at[shard(z - sign * (t - 1), rel), lo if h == 0 else hi]
        share(ref, h * 16 + side * 8 + (t - 1) * 2 + rel, z_to(sign), (h, side, t, rel))

    def across(side, t):
        zo = z + (t if side == 0 else -t)
        share(kt.at[shard(zo, 0), hi], 33 + side * 4 + t, y_to, ("y", side, t))

    share(kt.at[rows(me_r), lo], 32, y_to, "y")
    for side in (0, 1):
        forward(0, side, 1, 0)
        forward(1, side, 1, 0)
    across(0, 0)
    bc["y"].wait_recv()
    for side in (0, 1):
        forward(0, side, 1, 1)
    for t in range(2, 6):
        for h, rel in ((0, 0), (1, 0), (0, 1)):
            for side in (0, 1):
                if t - 1 > 4 - side:
                    continue
                bc[h, side, t - 1, rel].wait_recv()
                if t <= 4 - side:
                    forward(h, side, t, rel)
                if h == 1:
                    across(side, t - 1)
    for key in list(bc):
        if key != "y" and key[0] == "y":
            bc[key].wait_recv()
    tr = send(mine, kts.at[pl.ds(0, ch)], t_ss, t_rs, *t_out)
    tr.start()
    pending += [tr] + list(bc.values())

    cov_copy.wait()

    def product(sub):
        return jnp.dot(cov[rows(sub), :], kt[...], preferred_element_type=F32)

    def sub_of(k, cc):
        return cc * 8 + (g + k + 4) % 8

    def cx_copy(k):
        return send(cxs.at[k], cxr.at[k], cx_ss.at[k], cx_rs.at[k], *partner)

    def c_copy(k):
        return send(cs.at[k], cr.at[k], c_ss.at[k], c_rs.at[k], *g_to(k))

    def far(k):
        cxs[k] = product(sub_of(k, 1 - core)).astype(BF16)
        cx_copy(k).start()

    def near(k):
        v = product(sub_of(k, core))
        cx_copy(k).wait_recv()
        cs[k] = (v + cxr[k].astype(F32)).astype(BF16)
        c_copy(k).start()

    def step(k, carry):
        far((k + 3) % 8)
        near(k + 1)
        return carry

    far(1)
    far(2)
    lax.fori_loop(0, 6, step, 0)
    near(7)
    v = product(sub_of(0, core))
    cx_copy(0).wait_recv()
    v = v + cxr[0].astype(F32)
    for k in range(1, 8):
        c_copy(k).wait_recv()
        v = v + cr[k].astype(F32)
    v_hi = v.astype(BF16)
    v_lo = (v - v_hi.astype(F32)).astype(BF16)
    img_out[rows(own_sub), :] = v_hi

    tr.wait_recv()
    pad = jnp.zeros((kts.shape[0] - ch, kts.shape[1]), BF16)
    image_s = jnp.concatenate([v_hi, pad, v_lo, pad], 0)
    n2 = kts.shape[1] // 2

    def system_half(i):
        keys_s = kts[:, pl.ds(pl.multiple_of(i * n2, n2), n2)]
        return lax.dot_general(
            jnp.concatenate([keys_s, keys_s], 0), image_s, (((0,), (0,)), ((), ())),
            preferred_element_type=F32,
        )

    exs[...] = system_half(1 - core).astype(BF16)
    ex = send(exs, exr, ex_ss, ex_rs, *partner)
    ex.start()
    own_half = system_half(core)
    ex.wait_recv()
    e1s[...] = own_half + exr[...].astype(F32)
    blk = n2 // 8
    e1c = []
    for k in range(1, 8):
        e2s[k] = e1s[rows((g + k) % 8, blk), :].astype(BF16)
        cp = send(e2s.at[k], e1r.at[k], e1_ss.at[k], e1_rs.at[k], *g_to(k))
        cp.start()
        e1c.append(cp)
    dc = {}
    mine = img_out.at[rows(own_sub)]

    def gather(ref_of, ss, rs, out):
        for k in range(1, 8):
            ref = ref_of(g)
            out[k] = send(ref, ref, ss.at[k], rs.at[k], *g_to(k))
            out[k].start()
        ref = ref_of(g)
        out[0] = send(ref, ref, ss.at[0], rs.at[0], *partner)
        out[0].start()

    def relay(ref_of, ss, rs, out):
        for k in range(1, 8):
            out[k].wait_recv()
            ref = ref_of((g - k + 8) % 8)
            out[7 + k] = send(ref, ref, ss.at[7 + k], rs.at[7 + k], *partner)
            out[7 + k].start()

    def img_ref(gg):
        return img_out.at[rows(core * 8 + (gg + 4) % 8)]

    def s_ref(gg):
        return s_out.at[rows(core * 8 + gg, blk)]

    v = e1s[rows(g, blk), :]
    for k in range(1, 8):
        e1c[k - 1].wait_recv()
        v = v + e1r[k].astype(F32)
    s2[...] = v
    e1s[pl.ds(0, blk), :] = v
    tile = pl.ds(0, blk)

    def piece(ref, i):
        return ref.at[rows(i // 4, 8), pl.ds(pl.multiple_of(i % 4 * 128, 128), 128)]

    e2c = []
    for k in range(1, 16):
        cp = send(
            piece(e1s, (me_r + k) % 16), e2r.at[k], e2_ss.at[k], e2_rs.at[k],
            (me_r + k) % 16, me_c,
        )
        cp.start()
        e2c.append(cp)
    at_rows = rows(me_r // 4, 8)
    at_cols = pl.ds(pl.multiple_of(me_r % 4 * 128, 128), 128)
    v = e1s[at_rows, at_cols]
    for k in range(1, 16):
        e2c[k - 1].wait_recv()
        v = v + e2r[k]
    e3[...] = v
    e3c = []
    for k in range(1, 16):
        cp = send(
            e3, s2.at[at_rows, at_cols], e3_ss.at[k], e3_rs.at[k],
            (me_r + k) % 16, me_c,
        )
        cp.start()
        e3c.append(cp)
    s2[at_rows, at_cols] = v
    for cp in e3c:
        cp.wait_recv()
    s_out[rows(core * 8 + g, blk), :] = s2[...]
    ec = {}
    gather(s_ref, e4_ss, e4_rs, ec)
    relay(s_ref, e4_ss, e4_rs, ec)
    gather(img_ref, d_ss, d_rs, dc)
    ec[0].wait_recv()
    for k in range(1, 8):
        ec[7 + k].wait_recv()

    def d_relay(k):
        ref = img_ref((g - k + 8) % 8)
        return send(ref, ref, d_ss.at[7 + k], d_rs.at[7 + k], *partner)

    def relay_images():
        for k in range(1, 8):
            dc[k].wait_recv()
            d_relay(k).start()

    coeffs_out[...] = right_solve(s_out, work, pivot, target, relay_images)
    dc[0].wait_recv()
    for k in range(1, 8):
        d_relay(k).wait()
    pending += [ex] + e1c + e2c + e3c + list(ec.values()) + list(dc.values())
    for cp in pending:
        cp.wait_send()
    for k in range(8):
        cx_copy(k).wait_send()
    for k in range(1, 8):
        c_copy(k).wait_send()


def exchange(subject, target, gate_weight, up_weight, inv_cov):
    ff, facts = gate_weight.shape[1], subject.shape[1]
    ch, half, blk = ff // 16, facts // 2, facts // 16
    dma = pltpu.SemaphoreType.DMA
    vm = pltpu.VMEM
    scratch = [
        vm((facts, facts), F32), vm((facts, facts), F32),
        vm((facts // 4, facts // 4), F32), vm((2,) + gate_weight.shape, BF16),
        vm((2, ff, facts), F32), vm(inv_cov.shape, BF16),
        vm((8, 2, ch, half), BF16), vm((8, 2, ch, half), BF16),
        vm((7, 2, ch, half), BF16), vm((7, 2, ch, half), BF16),
        vm((7, 2, 2, ch, half), BF16), vm((7, 2, 2, ch, half), BF16),
        vm((2, ch, half), F32), vm((2, ch, half), F32),
        vm((ff, facts), BF16), vm((-(-ch // 128) * 128, facts), BF16),
        vm((8, ch, facts), BF16), vm((8, ch, facts), BF16),
        vm((8, ch, facts), BF16), vm((8, ch, facts), BF16),
        vm((facts // 2, facts), BF16), vm((facts // 2, facts), BF16),
        vm((facts // 2, facts), F32), vm((8, blk, facts), BF16),
        vm((8, blk, facts), BF16), vm((16, 8, 128), F32), vm((8, 128), F32),
        vm((blk, facts), F32),
        dma((2,)), dma(()), dma((8,)), dma((8,)), dma((24,)), dma((24,)), dma(()), dma(()),
        dma((41,)), dma((41,)), dma(()), dma(()),
        dma((8,)), dma((8,)), dma((8,)), dma((8,)), dma(()), dma(()),
        dma((8,)), dma((8,)), dma((16,)), dma((16,)), dma((16,)), dma((16,)),
        dma((15,)), dma((15,)), dma((15,)), dma((15,)), dma(()),
    ]
    return pl.pallas_call(
        exchange_kernel,
        name="exchange",
        out_shape=(
            jax.ShapeDtypeStruct(target.shape, BF16),
            jax.ShapeDtypeStruct((ff, facts), BF16),
        ),
        in_specs=[
            pl.BlockSpec(memory_space=pltpu.VMEM),
            pl.BlockSpec(memory_space=pltpu.VMEM),
            pl.BlockSpec(memory_space=pl.ANY),
            pl.BlockSpec(memory_space=pl.ANY),
            pl.BlockSpec(memory_space=pl.ANY),
        ],
        out_specs=[pl.BlockSpec(memory_space=pltpu.VMEM)] * 2,
        scratch_shapes=scratch,
        compiler_params=pltpu.CompilerParams(
            collective_id=0, has_side_effects=True, vmem_limit_bytes=60 * 2**20
        ),
    )(subject, target, gate_weight, up_weight, inv_cov)


def per_device(hidden, positions, gate_weight, up_weight, inv_cov, target_res):
    tokens = lax.broadcasted_iota(jnp.int32, (positions.shape[0], hidden.shape[0]), 1)
    chosen = (positions[:, None] == tokens).astype(BF16)
    subject = lax.dot_general(
        hidden, chosen, (((0,), (1,)), ((), ())), preferred_element_type=F32
    ).astype(BF16)
    coeffs, image_t = exchange(subject, target_res, gate_weight, up_weight, inv_cov)
    return lax.dot_general(
        coeffs, image_t, (((1,), (1,)), ((), ())), preferred_element_type=F32
    ).astype(BF16)


def solution(mesh):
    return jax.shard_map(
        per_device,
        mesh=mesh,
        in_specs=(
            P(None, "row"),
            P(),
            P("row", "col"),
            P("row", "col"),
            P("row", "col"),
            P("col", None),
        ),
        out_specs=P("col", "row"),
        check_vma=False,
    )
```

```python
import jax
import jax.numpy as jnp
from jax import lax
from jax.experimental import pallas as pl
from jax.experimental.pallas import tpu as pltpu
from jax.sharding import PartitionSpec as P

MESH = pl.DeviceIdType.MESH
F32 = jnp.float32
BF16 = jnp.bfloat16


def invert(m):
    n = m.shape[0]
    lane = lax.broadcasted_iota(jnp.int32, (1, n), 1)
    sub = lax.broadcasted_iota(jnp.int32, (8, 1), 0)
    for p in range(0, n, 4):
        row = [m[p + i : p + i + 1, :] for i in range(4)]
        col = [m[:, p + i : p + i + 1] for i in range(4)]

        def at(i, j):
            return jnp.broadcast_to(row[i][:, p + j : p + j + 1], (1, n))

        a, b, d = at(0, 0), at(0, 1), at(1, 1)
        r = 1.0 / (a * d - b * b)
        a, b, d = d * r, -b * r, a * r
        c = [[at(0, 2), at(0, 3)], [at(1, 2), at(1, 3)]]
        e = [[a * c[0][j] + b * c[1][j] for j in (0, 1)],
             [b * c[0][j] + d * c[1][j] for j in (0, 1)]]
        s0 = at(2, 2) - (c[0][0] * e[0][0] + c[1][0] * e[1][0])
        s1 = at(2, 3) - (c[0][0] * e[0][1] + c[1][0] * e[1][1])
        s2 = at(3, 3) - (c[0][1] * e[0][1] + c[1][1] * e[1][1])
        r = 1.0 / (s0 * s2 - s1 * s1)
        s0, s1, s2 = s2 * r, -s1 * r, s0 * r
        f = [[e[i][0] * s0 + e[i][1] * s1, e[i][0] * s1 + e[i][1] * s2] for i in (0, 1)]
        top = [[None, None], [None, None]]
        for i in (0, 1):
            for j in (0, 1):
                base = ((a, b), (b, d))[i][j]
                top[i][j] = base + f[i][0] * e[j][0] + f[i][1] * e[j][1]
        inv = [
            [top[0][0], top[0][1], -f[0][0], -f[0][1]],
            [top[1][0], top[1][1], -f[1][0], -f[1][1]],
            [-f[0][0], -f[1][0], s0, s1],
            [-f[0][1], -f[1][1], s1, s2],
        ]
        new = []
        for i in range(4):
            v = (inv[i][0] * row[0] + inv[i][1] * row[1]) + (
                inv[i][2] * row[2] + inv[i][3] * row[3]
            )
            for j in range(4):
                v = jnp.where(lane == p + j, inv[i][j], v)
            new.append(v)
        rest = jnp.where((lane >= p) & (lane < p + 4), 0.0, m)
        m = rest - (col[0] * new[0] + col[1] * new[1]) - (
            col[2] * new[2] + col[3] * new[3]
        )
        g0 = p // 8 * 8
        group = m[g0 : g0 + 8, :]
        for i in range(4):
            group = jnp.where(sub == p + i - g0, new[i], group)
        parts = [m[:g0, :]] * (g0 > 0) + [group] + [m[g0 + 8 :, :]] * (g0 + 8 < n)
        m = jnp.concatenate(parts, 0)
    return m


def right_solve(system, a, pivot, target, between):
    n = a.shape[0]
    b = n // 4
    eye = lax.broadcasted_iota(jnp.int32, (n, n), 0) == lax.broadcasted_iota(
        jnp.int32, (n, n), 1
    )
    a[...] = system[...] + jnp.where(eye, 1.0, 0.0)

    def dot(p, q):
        return jnp.dot(p, q, precision=lax.Precision.HIGHEST, preferred_element_type=F32)

    def block(k, carry):
        pl.when(k == 2)(between)
        d = pl.ds(pl.multiple_of(k * b, b), b)
        @pl.when(k < 4)
        def _():
            pivot[...] = invert(a[d, d])

        inv = pivot[...]
        col = a[:, d]
        wide = dot(inv, a[d, :])
        a[...] = a[...] - dot(col, wide)
        a[:, d] = -dot(col, inv)
        a[d, :] = wide
        a[d, d] = inv
        return carry

    lax.fori_loop(0, 4, block, 0)
    v = a[...]
    coeffs = jnp.zeros((target.shape[0], n), F32)
    for _ in range(3):
        short = v.astype(BF16)
        coeffs = coeffs + jnp.dot(target[...], short, preferred_element_type=F32)
        v = v - short.astype(F32)
    return coeffs.astype(BF16)


def exchange_kernel(
    subject, target_hbm, gate_hbm, up_hbm, cov_hbm, coeffs_out, img_out, s_out, work, pivot,
    target, weights, proj, cov, ysend, yrecv, psend, precv, qsend, qrecv, qy_s, qy_r,
    kt, kts, cxs, cxr, cs, cr, exs, exr, e1s, e1r, e2s, e2r, e3, s2,
    w_sem, cov_sem, y_ss, y_rs, z_ss, z_rs, qy_ss, qy_rs, b_ss, b_rs, t_ss, t_rs,
    cx_ss, cx_rs, c_ss, c_rs, ex_ss, ex_rs, e1_ss, e1_rs, e2_ss, e2_rs,
    e3_ss, e3_rs, e4_ss, e4_rs, d_ss, d_rs, loc_sem,
):
    ch = kt.shape[0] // 16
    half = kt.shape[1] // 2
    me_r, me_c = lax.axis_index("row"), lax.axis_index("col")
    y, z = me_r // 8, me_r % 8
    g, core = me_c // 2, me_c % 2

    def send(src, dst, ss, rs, r, c):
        return pltpu.make_async_remote_copy(
            src_ref=src, dst_ref=dst, send_sem=ss, recv_sem=rs,
            device_id=(r, c), device_id_type=MESH,
        )

    def rows(i, n=ch):
        return pl.ds(pl.multiple_of(i * n, 8), n)

    y_to = ((1 - y) * 8 + z, me_c)

    def z_to(step):
        return (y * 8 + (z + step + 8) % 8, me_c)

    partner = (me_r, g * 2 + 1 - core)

    def g_to(k):
        return (me_r, ((g + k) % 8) * 2 + core)

    own_sub = core * 8 + (g + 4) % 8
    t_out = (me_c, ((me_r % 8 + 4) % 8) * 2 + me_r // 8)
    t_in = (own_sub, me_r)

    loads = [
        pltpu.make_async_copy(gate_hbm, weights.at[0], w_sem.at[0]),
        pltpu.make_async_copy(up_hbm, weights.at[1], w_sem.at[1]),
    ]
    cov_copy = pltpu.make_async_copy(cov_hbm, cov, cov_sem)
    target_copy = pltpu.make_async_copy(target_hbm, target, w_sem.at[2])
    for cp in loads:
        cp.start()

    kts[...] = jnp.zeros_like(kts)
    barrier = pltpu.get_barrier_semaphore()
    peers = [((me_r + k) % 16, me_c) for k in range(1, 16)]
    peers += [g_to(k) for k in range(1, 8)] + [partner, t_out, t_in]
    for p in peers:
        pl.semaphore_signal(barrier, inc=1, device_id=p, device_id_type=MESH)
    lo, hi = pl.ds(0, half), pl.ds(half, half)
    pending = []
    width = proj.shape[1] // 7

    def project(i):
        def step(j, carry):
            at = pl.ds(pl.multiple_of(j * width, width), width)
            proj[i, at, :] = lax.dot_general(
                weights[i, :, at], subject[...], (((0,), (0,)), ((), ())),
                preferred_element_type=F32,
            )
            return carry

        loads[i].wait()
        lax.fori_loop(0, 7, step, 0)

    project(0)
    cov_copy.start()
    target_copy.start()
    project(1)

    def projections(r, lanes):
        return proj[:, rows(r), lanes]

    order = (4, 3, 5, 2, 6, 1, 7, 0)
    for o in order:
        ysend[o] = projections((1 - y) * 8 + (z + o) % 8, lo).astype(BF16)
    pl.semaphore_wait(barrier, len(peers))
    ycopies = {}
    for o in order:
        ycopies[o] = send(ysend.at[o], yrecv.at[o], y_ss.at[o], y_rs.at[o], *y_to)
        ycopies[o].start()

    def p_own(o):
        return projections(y * 8 + (z + o) % 8, lo) + yrecv[o].astype(F32)

    def q_own(o, yy):
        return projections(yy * 8 + (z + o) % 8, hi)

    copies = {}
    for s in range(1, 5):
        for chain in range(3):
            for side in (0, 1):
                if side == 1 and s == 1:
                    continue
                slot = side * 4 + s - 1 - side
                sign = (-1 if side == 0 else 1) * (-1 if chain == 2 else 1)
                o = (sign * (5 - s)) % 8
                if chain == 2:
                    ycopies[o].wait_recv()
                    v = p_own(o)
                    src, dst = psend.at[slot], precv
                else:
                    v = q_own(o, chain)
                    src, dst = qsend.at[slot, chain], qrecv.at[:, chain]
                if s > 1 + side:
                    copies[chain, side, s - 1].wait_recv()
                    v = v + dst[slot - 1].astype(F32)
                src[...] = v.astype(BF16)
                i = chain * 8 + side * 4 + s - 1
                cp = send(src, dst.at[slot], z_ss.at[i], z_rs.at[i], *z_to(sign))
                cp.start()
                copies[chain, side, s] = cp
    for chain in (0, 1):
        copies[chain, 0, 4].wait_recv()
        copies[chain, 1, 4].wait_recv()

    def q_sum(yy):
        return q_own(0, yy) + qrecv[3, yy].astype(F32) + qrecv[6, yy].astype(F32)

    qy_s[...] = q_sum(1 - y)
    qy = send(qy_s, qy_r, qy_ss, qy_rs, *y_to)
    qy.start()
    ycopies[0].wait_recv()
    copies[2, 0, 4].wait_recv()
    copies[2, 1, 4].wait_recv()
    v = p_own(0) + precv[3].astype(F32) + precv[6].astype(F32)
    kt[rows(me_r), lo] = (v[0] / (1.0 + jnp.exp(-v[0])) * v[1]).astype(BF16)
    v = q_sum(y)
    qy.wait_recv()
    v = v + qy_r[...]
    kt[rows(me_r), hi] = (v[0] / (1.0 + jnp.exp(-v[0])) * v[1]).astype(BF16)
    pending += list(ycopies.values()) + list(copies.values()) + [qy]

    def shard(zo, rel):
        yy = y if rel == 0 else 1 - y
        return rows(yy * 8 + (zo + 8) % 8)

    mine = kt.at[rows(me_r)]
    bc = {}

    def share(ref, i, to, key):
        bc[key] = send(ref, ref, b_ss.at[i], b_rs.at[i], *to)
        bc[key].start()

    def forward(h, side, t, rel):
        sign = 1 if h == side else -1
        ref = kt.at[shard(z - sign * (t - 1), rel), lo if h == 0 else hi]
        share(ref, h * 16 + side * 8 + (t - 1) * 2 + rel, z_to(sign), (h, side, t, rel))

    def across(side, t):
        zo = z + (t if side == 0 else -t)
        share(kt.at[shard(zo, 0), hi], 33 + side * 4 + t, y_to, ("y", side, t))

    share(kt.at[rows(me_r), lo], 32, y_to, "y")
    for side in (0, 1):
        forward(0, side, 1, 0)
        forward(1, side, 1, 0)
    across(0, 0)
    bc["y"].wait_recv()
    for side in (0, 1):
        forward(0, side, 1, 1)
    for t in range(2, 6):
        for h, rel in ((0, 0), (1, 0), (0, 1)):
            for side in (0, 1):
                if t - 1 > 4 - side:
                    continue
                bc[h, side, t - 1, rel].wait_recv()
                if t <= 4 - side:
                    forward(h, side, t, rel)
                if h == 1:
                    across(side, t - 1)
    for key in list(bc):
        if key != "y" and key[0] == "y":
            bc[key].wait_recv()
    tr = send(mine, kts.at[pl.ds(0, ch)], t_ss, t_rs, *t_out)
    tr.start()
    pending += [tr] + list(bc.values())

    cov_copy.wait()

    def product(sub):
        return jnp.dot(cov[rows(sub), :], kt[...], preferred_element_type=F32)

    def sub_of(k, cc):
        return cc * 8 + (g + k + 4) % 8

    def cx_copy(k):
        return send(cxs.at[k], cxr.at[k], cx_ss.at[k], cx_rs.at[k], *partner)

    def c_copy(k):
        return send(cs.at[k], cr.at[k], c_ss.at[k], c_rs.at[k], *g_to(k))

    def far(k):
        cxs[k] = product(sub_of(k, 1 - core)).astype(BF16)
        cx_copy(k).start()

    def near(k):
        v = product(sub_of(k, core))
        cx_copy(k).wait_recv()
        cs[k] = (v + cxr[k].astype(F32)).astype(BF16)
        c_copy(k).start()

    def step(k, carry):
        far((k + 3) % 8)
        near(k + 1)
        return carry

    far(1)
    far(2)
    lax.fori_loop(0, 6, step, 0)
    near(7)
    v = product(sub_of(0, core))
    cx_copy(0).wait_recv()
    v = v + cxr[0].astype(F32)
    for k in range(1, 8):
        c_copy(k).wait_recv()
        v = v + cr[k].astype(F32)
    v_hi = v.astype(BF16)
    v_lo = (v - v_hi.astype(F32)).astype(BF16)
    img_out[rows(own_sub), :] = v_hi

    tr.wait_recv()
    pad = jnp.zeros((kts.shape[0] - ch, kts.shape[1]), BF16)
    image_s = jnp.concatenate([v_hi, pad, v_lo, pad], 0)
    n2 = kts.shape[1] // 2

    def system_half(i):
        keys_s = kts[:, pl.ds(pl.multiple_of(i * n2, n2), n2)]
        return lax.dot_general(
            jnp.concatenate([keys_s, keys_s], 0), image_s, (((0,), (0,)), ((), ())),
            preferred_element_type=F32,
        )

    exs[...] = system_half(1 - core).astype(BF16)
    ex = send(exs, exr, ex_ss, ex_rs, *partner)
    ex.start()
    own_half = system_half(core)
    ex.wait_recv()
    e1s[...] = own_half + exr[...].astype(F32)
    blk = n2 // 8
    e1c = []
    for k in range(1, 8):
        e2s[k] = e1s[rows((g + k) % 8, blk), :].astype(BF16)
        cp = send(e2s.at[k], e1r.at[k], e1_ss.at[k], e1_rs.at[k], *g_to(k))
        cp.start()
        e1c.append(cp)
    dc = {}
    mine = img_out.at[rows(own_sub)]

    def gather(ref_of, ss, rs, out):
        for k in range(1, 8):
            ref = ref_of(g)
            out[k] = send(ref, ref, ss.at[k], rs.at[k], *g_to(k))
            out[k].start()
        ref = ref_of(g)
        out[0] = send(ref, ref, ss.at[0], rs.at[0], *partner)
        out[0].start()

    def relay(ref_of, ss, rs, out):
        for k in range(1, 8):
            out[k].wait_recv()
            ref = ref_of((g - k + 8) % 8)
            out[7 + k] = send(ref, ref, ss.at[7 + k], rs.at[7 + k], *partner)
            out[7 + k].start()

    def img_ref(gg):
        return img_out.at[rows(core * 8 + (gg + 4) % 8)]

    def s_ref(gg):
        return s_out.at[rows(core * 8 + gg, blk)]

    v = e1s[rows(g, blk), :]
    for k in range(1, 8):
        e1c[k - 1].wait_recv()
        v = v + e1r[k].astype(F32)
    s2[...] = v
    e1s[pl.ds(0, blk), :] = v
    tile = pl.ds(0, blk)

    def piece(ref, i):
        return ref.at[rows(i // 4, 8), pl.ds(pl.multiple_of(i % 4 * 128, 128), 128)]

    e2c = []
    for k in range(1, 16):
        cp = send(
            piece(e1s, (me_r + k) % 16), e2r.at[k], e2_ss.at[k], e2_rs.at[k],
            (me_r + k) % 16, me_c,
        )
        cp.start()
        e2c.append(cp)
    at_rows = rows(me_r // 4, 8)
    at_cols = pl.ds(pl.multiple_of(me_r % 4 * 128, 128), 128)
    v = e1s[at_rows, at_cols]
    for k in range(1, 16):
        e2c[k - 1].wait_recv()
        v = v + e2r[k]
    e3[...] = v
    e3c = []
    for k in range(1, 16):
        cp = send(
            e3, s2.at[at_rows, at_cols], e3_ss.at[k], e3_rs.at[k],
            (me_r + k) % 16, me_c,
        )
        cp.start()
        e3c.append(cp)
    s2[at_rows, at_cols] = v
    for cp in e3c:
        cp.wait_recv()
    s_out[rows(core * 8 + g, blk), :] = s2[...]
    ec = {}
    gather(s_ref, e4_ss, e4_rs, ec)
    relay(s_ref, e4_ss, e4_rs, ec)
    gather(img_ref, d_ss, d_rs, dc)
    ec[0].wait_recv()
    for k in range(1, 8):
        ec[7 + k].wait_recv()

    def d_relay(k):
        ref = img_ref((g - k + 8) % 8)
        return send(ref, ref, d_ss.at[7 + k], d_rs.at[7 + k], *partner)

    def relay_images():
        for k in range(1, 8):
            dc[k].wait_recv()
            d_relay(k).start()

    target_copy.wait()
    coeffs_out[...] = right_solve(s_out, work, pivot, target, relay_images)
    dc[0].wait_recv()
    for k in range(1, 8):
        d_relay(k).wait()
    pending += [ex] + e1c + e2c + e3c + list(ec.values()) + list(dc.values())
    for cp in pending:
        cp.wait_send()
    for k in range(8):
        cx_copy(k).wait_send()
    for k in range(1, 8):
        c_copy(k).wait_send()


def exchange(subject, target, gate_weight, up_weight, inv_cov):
    ff, facts = gate_weight.shape[1], subject.shape[1]
    ch, half, blk = ff // 16, facts // 2, facts // 16
    dma = pltpu.SemaphoreType.DMA
    vm = pltpu.VMEM
    scratch = [
        vm((facts, facts), F32), vm((facts, facts), F32),
        vm((facts // 4, facts // 4), F32), vm(target.shape, BF16), vm((2,) + gate_weight.shape, BF16),
        vm((2, ff, facts), F32), vm(inv_cov.shape, BF16),
        vm((8, 2, ch, half), BF16), vm((8, 2, ch, half), BF16),
        vm((7, 2, ch, half), BF16), vm((7, 2, ch, half), BF16),
        vm((7, 2, 2, ch, half), BF16), vm((7, 2, 2, ch, half), BF16),
        vm((2, ch, half), F32), vm((2, ch, half), F32),
        vm((ff, facts), BF16), vm((-(-ch // 128) * 128, facts), BF16),
        vm((8, ch, facts), BF16), vm((8, ch, facts), BF16),
        vm((8, ch, facts), BF16), vm((8, ch, facts), BF16),
        vm((facts // 2, facts), BF16), vm((facts // 2, facts), BF16),
        vm((facts // 2, facts), F32), vm((8, blk, facts), BF16),
        vm((8, blk, facts), BF16), vm((16, 8, 128), F32), vm((8, 128), F32),
        vm((blk, facts), F32),
        dma((3,)), dma(()), dma((8,)), dma((8,)), dma((24,)), dma((24,)), dma(()), dma(()),
        dma((41,)), dma((41,)), dma(()), dma(()),
        dma((8,)), dma((8,)), dma((8,)), dma((8,)), dma(()), dma(()),
        dma((8,)), dma((8,)), dma((16,)), dma((16,)), dma((16,)), dma((16,)),
        dma((15,)), dma((15,)), dma((15,)), dma((15,)), dma(()),
    ]
    return pl.pallas_call(
        exchange_kernel,
        name="exchange",
        out_shape=(
            jax.ShapeDtypeStruct(target.shape, BF16),
            jax.ShapeDtypeStruct((ff, facts), BF16),
        ),
        in_specs=[
            pl.BlockSpec(memory_space=pltpu.VMEM),
            pl.BlockSpec(memory_space=pl.ANY),
            pl.BlockSpec(memory_space=pl.ANY),
            pl.BlockSpec(memory_space=pl.ANY),
            pl.BlockSpec(memory_space=pl.ANY),
        ],
        out_specs=[pl.BlockSpec(memory_space=pltpu.VMEM)] * 2,
        scratch_shapes=scratch,
        compiler_params=pltpu.CompilerParams(
            collective_id=0, has_side_effects=True, vmem_limit_bytes=60 * 2**20
        ),
    )(subject, target, gate_weight, up_weight, inv_cov)


def per_device(hidden, positions, gate_weight, up_weight, inv_cov, target_res):
    tokens = lax.broadcasted_iota(jnp.int32, (positions.shape[0], hidden.shape[0]), 1)
    chosen = (positions[:, None] == tokens).astype(BF16)
    subject = lax.dot_general(
        hidden, chosen, (((0,), (1,)), ((), ())), preferred_element_type=F32
    ).astype(BF16)
    coeffs, image_t = exchange(subject, target_res, gate_weight, up_weight, inv_cov)
    return lax.dot_general(
        coeffs, image_t, (((1,), (1,)), ((), ())), preferred_element_type=F32
    ).astype(BF16)


def solution(mesh):
    return jax.shard_map(
        per_device,
        mesh=mesh,
        in_specs=(
            P(None, "row"),
            P(),
            P("row", "col"),
            P("row", "col"),
            P("row", "col"),
            P("col", None),
        ),
        out_specs=P("col", "row"),
        check_vma=False,
    )
```
